32 devices in a mesh: dp: 8 (over z, y), expert: 4 (over x, core).
Axes of the slice: x: 2, y: 2, z: 4, core: 2. Of those that a mesh axis runs over, the one named last changes fastest.
Arguments:
- tokens: bfloat16 [512, 2048], P(('dp', 'expert')), may hold values from -6 to 6
- expert_ids: int32 [512, 8], P(('dp', 'expert')), may hold values from 0 to 15, as said below
- route_weight: float32 [512, 8], P(('dp', 'expert')), may hold values from 0.03 to 0.6
- out_grad: bfloat16 [512, 2048], P(('dp', 'expert')), may hold values from -6 to 6
- gate_weight: bfloat16 [32, 2048, 384], P(('dp', 'expert')), may hold values from -0.125 to 0.125
- up_weight: bfloat16 [32, 2048, 384], P(('dp', 'expert')), may hold values from -0.125 to 0.125
- down_weight: bfloat16 [32, 384, 2048], P(('dp', 'expert')), may hold values from -0.21875 to 0.21875
Outputs:
- layer_out: bfloat16 [512, 2048], P(('dp', 'expert'))
- token_grad: bfloat16 [512, 2048], P(('dp', 'expert'))
- route_grad: float32 [512, 8], P(('dp', 'expert'))
- gate_grad: bfloat16 [32, 2048, 384], P(('dp', 'expert'))
- up_grad: bfloat16 [32, 2048, 384], P(('dp', 'expert'))
- down_grad: bfloat16 [32, 384, 2048], P(('dp', 'expert'))
The draws below stay inside these ranges and needn't reach their ends.
Inputs may be any that keep to these rules, and one draw needn't show every extreme that they name: `expert_ids`: each row names 8 different experts. The rows of one device name no expert more than 16 times, and one expert is named exactly 16 times by the rows of every device.
All inputs are finite; a program needn't handle non-finite values.
Results may differ from the reference program's by a relative error of at most 0.0071.
Values may be sent and summed in bfloat16 or wider, within the bound.
A program may use at most 128 MiB of HBM per device.

```python
import math
import jax
import jax.numpy as jnp
from jax import lax

D = 2048
FF = 768
TOP = 8
TOK_DEV = 16
HALF = 384
EXPERTS = 16
CAP = 16
TOKENS = 512
DEVICES = 32


def shuffle_experts(subkey):
    return jax.random.permutation(subkey, EXPERTS - 1)


def shuffle_rows(subkey):
    return jax.random.permutation(subkey, TOK_DEV)


def draw_expert_ids(key, part):
    base_key = jax.random.fold_in(key, 7)
    key_hot, key_width, key_perm, key_rows, key_turn = jax.random.split(base_key, 5)
    blocks = TOKENS // TOK_DEV
    hot_expert = jax.random.randint(key_hot, (), 0, EXPERTS)
    widths = jax.random.randint(key_width, (blocks,), EXPERTS // 2, EXPERTS)
    orders = jax.vmap(shuffle_experts)(jax.random.split(key_perm, blocks))
    others = orders + (orders >= hot_expert).astype(jnp.int32)
    row_ids = jnp.arange(TOK_DEV, dtype=jnp.int32)[:, None]
    pick_ids = jnp.arange(TOP, dtype=jnp.int32)[None, :]
    hot_slot = (row_ids < CAP) & (pick_ids == 0)
    earlier = jnp.minimum(row_ids, CAP) + ((row_ids < CAP) & (pick_ids > 0)).astype(jnp.int32)
    running = row_ids * TOP + pick_ids - earlier
    position = running[None, :, :] % widths[:, None, None]
    chosen = jnp.take_along_axis(others, position.reshape(blocks, TOK_DEV * TOP), axis=1).reshape(blocks, TOK_DEV, TOP)
    routed = jnp.where(hot_slot[None, :, :], hot_expert, chosen)
    row_perm = jax.vmap(shuffle_rows)(jax.random.split(key_rows, blocks))
    routed = jnp.take_along_axis(routed, row_perm[:, :, None], axis=1)
    rotation = jax.random.randint(key_turn, (blocks, TOK_DEV, 1), 0, TOP)
    routed = jnp.take_along_axis(routed, (pick_ids[None, :, :] + rotation) % TOP, axis=2)
    return routed.reshape(TOKENS, TOP).astype(jnp.int32)


def block_levels(key, extent, cuts, least, largest):
    gain = 1.0
    for axis_at, parts in cuts:
        heights = jax.random.uniform(jax.random.fold_in(jax.random.fold_in(key, 6), axis_at), (parts,), jnp.float32, least / len(cuts), largest / len(cuts))
        gain = gain * jnp.repeat(jnp.exp(heights), extent[axis_at] // parts).reshape((-1,) + (1,) * (len(extent) - 1 - axis_at))
    return gain


def noise(own_key, dims, deviation, limit, cuts=(), kind=jnp.bfloat16):
    entries = jax.random.normal(own_key, dims, jnp.float32) * deviation
    if len(cuts) > 0:
        entries = block_levels(own_key, dims, cuts, -0.22, 0.18) * entries
    return jnp.clip(entries, min=-limit, max=limit).astype(kind)


def setup_inputs(seed: int = 0) -> dict:
    key_of = jax.random.split(jax.random.key(seed), 8)
    tokens = noise(key_of[0], (TOKENS, D), 1.0, 6.0, ((0, 32),))
    expert_ids = draw_expert_ids(jax.random.fold_in(key_of[7], 71), 0)
    route_weight = jnp.clip(jnp.exp(math.log(0.6) - 2.9957323 * jax.random.uniform(key_of[2], (TOKENS, TOP), jnp.float32) ** block_levels(key_of[2], (TOKENS, TOP), ((0, 32),), -0.2, 0.2)), 0.03, 0.6)
    out_grad = noise(key_of[3], (TOKENS, D), 1.0, 6.0, ((0, 32),))
    gate_weight = noise(key_of[4], (DEVICES, D, HALF), D ** -0.5, 0.125, ((0, 32),))
    up_weight = noise(key_of[5], (DEVICES, D, HALF), D ** -0.5, 0.125, ((0, 32),))
    down_weight = noise(key_of[6], (DEVICES, HALF, D), FF ** -0.5, 0.21875, ((0, 32),))
    return dict(tokens=tokens, expert_ids=expert_ids, route_weight=route_weight, out_grad=out_grad, gate_weight=gate_weight, up_weight=up_weight, down_weight=down_weight)


def reference(tokens, expert_ids, route_weight, out_grad, gate_weight, up_weight, down_weight):
    tok_total = tokens.shape[0]
    assigned = tok_total * TOP
    flat_ids = expert_ids.reshape(-1).astype(jnp.int32)
    per_block = flat_ids.reshape(-1, TOK_DEV * TOP)
    onehot = (per_block[:, :, None] == jnp.arange(EXPERTS, dtype=jnp.int32)[None, None, :]).astype(jnp.int32)
    before = jnp.cumsum(onehot, axis=1) - onehot
    slot_ids = jnp.sum(before * onehot, axis=2).reshape(-1).astype(jnp.int32)
    device_ids = jnp.arange(assigned, dtype=jnp.int32) // (TOK_DEV * TOP)
    place_row = ((flat_ids * DEVICES + device_ids) * CAP + slot_ids).astype(jnp.int32)
    slot_table = jnp.full((EXPERTS * DEVICES * CAP,), -1, jnp.int32).at[place_row].set(jnp.arange(assigned, dtype=jnp.int32))
    slot_table = slot_table.reshape(EXPERTS, DEVICES * CAP)
    weights_flat = route_weight.reshape(-1)

    def expert_step(accum, expert):
        out_acc, grad_acc, route_acc = accum
        entry_ids = slot_table[expert]
        filled = entry_ids >= 0
        assign = jnp.maximum(entry_ids, 0)
        tok_rows = assign // TOP
        in_rows = jnp.where(filled[:, None], tokens[tok_rows], jnp.zeros((), jnp.bfloat16))
        weight_rows = jnp.where(filled, weights_flat[assign], jnp.zeros((), jnp.float32))
        grad_rows = out_grad[tok_rows].astype(jnp.float32)
        scaled = (weight_rows[:, None] * grad_rows).astype(jnp.bfloat16)
        partials = []
        partial_grads = []
        gate_pieces = []
        up_pieces = []
        down_pieces = []
        for piece_half in range(2):
            piece_id = 2 * expert + piece_half
            w_gate = gate_weight[piece_id]
            w_up = up_weight[piece_id]
            w_down = down_weight[piece_id]
            gate_act = jnp.dot(in_rows, w_gate, preferred_element_type=jnp.float32)
            up_act = jnp.dot(in_rows, w_up, preferred_element_type=jnp.float32)
            sig_gate = jax.nn.sigmoid(gate_act)
            hidden = (gate_act * sig_gate * up_act).astype(jnp.bfloat16)
            partials.append(jnp.dot(hidden, w_down, preferred_element_type=jnp.float32).astype(jnp.bfloat16))
            hidden_grad = jnp.dot(scaled, w_down.T, preferred_element_type=jnp.float32)
            gate_pre = (hidden_grad * up_act * sig_gate * (1.0 + gate_act * (1.0 - sig_gate))).astype(jnp.bfloat16)
            up_pre = (hidden_grad * gate_act * sig_gate).astype(jnp.bfloat16)
            partial_grads.append((jnp.dot(gate_pre, w_gate.T, preferred_element_type=jnp.float32) + jnp.dot(up_pre, w_up.T, preferred_element_type=jnp.float32)).astype(jnp.bfloat16))
            gate_pieces.append(jnp.dot(in_rows.T, gate_pre, preferred_element_type=jnp.float32).astype(jnp.bfloat16))
            up_pieces.append(jnp.dot(in_rows.T, up_pre, preferred_element_type=jnp.float32).astype(jnp.bfloat16))
            down_pieces.append(jnp.dot(hidden.T, scaled, preferred_element_type=jnp.float32).astype(jnp.bfloat16))
        expert_out = (partials[0].astype(jnp.float32) + partials[1].astype(jnp.float32)).astype(jnp.bfloat16)
        out_acc = out_acc.at[tok_rows].add(weight_rows[:, None] * expert_out.astype(jnp.float32))
        route_term = jnp.sum(grad_rows * expert_out.astype(jnp.float32), axis=1)
        route_acc = route_acc.at[assign].add(jnp.where(filled, route_term, jnp.zeros((), jnp.float32)))
        expert_grad = (partial_grads[0].astype(jnp.float32) + partial_grads[1].astype(jnp.float32)).astype(jnp.bfloat16)
        grad_acc = grad_acc.at[tok_rows].add(jnp.where(filled[:, None], expert_grad.astype(jnp.float32), jnp.zeros((), jnp.float32)))
        return (out_acc, grad_acc, route_acc), (jnp.stack(gate_pieces), jnp.stack(up_pieces), jnp.stack(down_pieces))

    start = (jnp.zeros((tok_total, D), jnp.float32), jnp.zeros((tok_total, D), jnp.float32), jnp.zeros((assigned,), jnp.float32))
    final, stacked = lax.scan(expert_step, start, jnp.arange(EXPERTS, dtype=jnp.int32))
    out_acc, grad_acc, route_acc = final
    gate_all, up_all, down_all = stacked
    return (out_acc.astype(jnp.bfloat16), grad_acc.astype(jnp.bfloat16), route_acc.reshape(tok_total, TOP),
            gate_all.reshape(DEVICES, D, HALF), up_all.reshape(DEVICES, D, HALF), down_all.reshape(DEVICES, HALF, D))
```

```python
import functools

import jax
import jax.numpy as jnp
from jax import lax
from jax.experimental import pallas as pl
from jax.experimental.pallas import tpu as pltpu
from jax.sharding import PartitionSpec as P

LANES = 128
TILE = 256
PARTS = 4
WIDE = (512, 384)
THIN = (256, 256)


def from_partner(shard, axis, apart):
    return lax.ppermute(shard, axis, [(i, i ^ 1 << apart) for i in range(lax.axis_size(axis))])


def contract(left_op, right_op, left_dim, right_dim):
    return lax.dot_general(
        left_op,
        right_op,
        (((left_dim,), (right_dim,)), ((), ())),
        preferred_element_type=jnp.float32,
    )


def deliver(buffer, dp_size, ex_size, experts, capacity, backward):
    feat_width = buffer.shape[1]
    doubled = jnp.broadcast_to(
        buffer.reshape(experts, 1, capacity, feat_width), (experts, 2, capacity, feat_width)
    )
    doubled = doubled.reshape(dp_size, ex_size, capacity, feat_width)
    if backward:
        arrived = lax.all_to_all(
            lax.all_to_all(doubled, "dp", split_axis=0, concat_axis=0, tiled=True),
            "expert",
            split_axis=1,
            concat_axis=1,
            tiled=True,
        )
    else:
        arrived = lax.all_to_all(
            lax.all_to_all(doubled, "dp", split_axis=0, concat_axis=0, tiled=True),
            "expert",
            split_axis=1,
            concat_axis=1,
            tiled=True,
        )
    return arrived.reshape(-1, feat_width)


def bring_back(partials_in, dp_size, ex_size, experts, capacity, half_index, backward):
    feat_width = partials_in.shape[1]
    if backward:
        partner = from_partner(partials_in, "expert", 0)
    else:
        partner = from_partner(partials_in, "expert", 0)
    summed = (partials_in.astype(jnp.float32) + partner.astype(jnp.float32)).astype(jnp.bfloat16)
    summed = summed.reshape(dp_size, ex_size, capacity, feat_width)
    own_half = lax.dynamic_slice_in_dim(summed, half_index * (capacity // 2), capacity // 2, 2)
    if backward:
        returned = lax.all_to_all(
            lax.all_to_all(own_half, "dp", split_axis=0, concat_axis=0, tiled=True),
            "expert",
            split_axis=1,
            concat_axis=1,
            tiled=True,
        )
    else:
        returned = lax.all_to_all(
            lax.all_to_all(own_half, "dp", split_axis=0, concat_axis=0, tiled=True),
            "expert",
            split_axis=1,
            concat_axis=1,
            tiled=True,
        )
    merged = returned.reshape(experts, capacity, feat_width)
    return merged.reshape(experts * capacity, feat_width)


def body(tokens, expert_ids, route_weight, out_grad, gate_weight, up_weight, down_weight):
    dp_size = lax.axis_size("dp")
    ex_size = lax.axis_size("expert")
    tok_count, feat_width = tokens.shape
    top_count = expert_ids.shape[1]
    experts = dp_size * ex_size // 2
    assigned = tok_count * top_count
    capacity = 2 * (assigned // experts)
    half_index = lax.axis_index("expert") % 2
    flat_ids = expert_ids.reshape(-1)
    order = jnp.arange(assigned, dtype=jnp.int32)
    earlier = (flat_ids[:, None] == flat_ids[None, :]) & (order[None, :] < order[:, None])
    slot_ids = jnp.sum(earlier.astype(jnp.int32), axis=1)
    place_row = flat_ids * capacity + slot_ids
    source = (
        jnp.full((experts * capacity,), -1, jnp.int32)
        .at[place_row]
        .set(jnp.arange(assigned, dtype=jnp.int32))
    )
    filled = source >= 0
    assign = jnp.maximum(source, 0)
    rows_tok = assign // top_count
    send_rows = jnp.where(filled[:, None], tokens[rows_tok], jnp.zeros((), jnp.bfloat16))
    in_rows = deliver(send_rows, dp_size, ex_size, experts, capacity, False)
    w_gate = gate_weight[0]
    w_up = up_weight[0]
    w_down = down_weight[0]
    gate_act = jnp.dot(in_rows, w_gate, preferred_element_type=jnp.float32)
    up_act = jnp.dot(in_rows, w_up, preferred_element_type=jnp.float32)
    sig_gate = jax.nn.sigmoid(gate_act)
    hidden = (gate_act * sig_gate * up_act).astype(jnp.bfloat16)
    partial_value = jnp.dot(hidden, w_down, preferred_element_type=jnp.float32).astype(jnp.bfloat16)
    expert_table = bring_back(partial_value, dp_size, ex_size, experts, capacity, half_index, False)
    expert_rows = expert_table[place_row].reshape(tok_count, top_count, feat_width)
    layer_out = jnp.sum(route_weight[:, :, None] * expert_rows.astype(jnp.float32), axis=1).astype(
        jnp.bfloat16
    )
    route_grad = jnp.einsum("tkd,td->tk", expert_rows, out_grad, preferred_element_type=jnp.float32)
    scaled = (route_weight[:, :, None] * out_grad[:, None, :].astype(jnp.float32)).astype(
        jnp.bfloat16
    )
    scaled = scaled.reshape(assigned, feat_width)
    send_grad = jnp.where(filled[:, None], scaled[assign], jnp.zeros((), jnp.bfloat16))
    grad_rows = deliver(send_grad, dp_size, ex_size, experts, capacity, True)
    hidden_grad = contract(grad_rows, w_down, 1, 1)
    gate_pre = (hidden_grad * up_act * sig_gate * (1.0 + gate_act * (1.0 - sig_gate))).astype(
        jnp.bfloat16
    )
    up_pre = (hidden_grad * gate_act * sig_gate).astype(jnp.bfloat16)
    partial_grad = (contract(gate_pre, w_gate, 1, 1) + contract(up_pre, w_up, 1, 1)).astype(
        jnp.bfloat16
    )
    gate_grad = contract(in_rows, gate_pre, 0, 0).astype(jnp.bfloat16)
    up_grad = contract(in_rows, up_pre, 0, 0).astype(jnp.bfloat16)
    down_grad = contract(hidden, grad_rows, 0, 0).astype(jnp.bfloat16)
    grad_table = bring_back(partial_grad, dp_size, ex_size, experts, capacity, half_index, True)
    expert_grad = grad_table[place_row].reshape(tok_count, top_count, feat_width)
    token_grad = jnp.sum(expert_grad.astype(jnp.float32), axis=1).astype(jnp.bfloat16)
    return (layer_out, token_grad, route_grad, gate_grad[None], up_grad[None], down_grad[None])


def expert_kernel(
    planes, tok_count, width, half, experts, tile, wide, thin,
    tok_hbm, ids_hbm, rw_hbm, og_hbm, wg_hbm, wu_hbm, wd_hbm,
    lo_ref, tg_ref, rg_ref, gg_ref, ug_ref, dg_ref,
    ids_ref, rw_ref, rows, parts, swapped, summed, early, first_a, first_b, turn_a, turn_b, second_a, second_b,
    zsend, zrecv, zown, hidden_all, pre_all, wg_ref, wu_ref, wd_ref,
    load_sem, z_ss, z_rs, x_ss, x_rs, y_ss, y_rs, xh_ss, xh_rs, yh_ss, yh_rs, wide_ss, wide_rs,
    core_ss, core_rs, swap_ss, swap_rs, early_ss, early_rs, fa_ss, fa_rs, fb_ss, fb_rs,
    ta_ss, ta_rs, tb_ss, tb_rs, zo_ss, zo_rs,
):
    f32, bf16 = jnp.float32, jnp.bfloat16
    dp, ex = lax.axis_index("dp"), lax.axis_index("expert")
    z, y, x, c = dp // 2, dp % 2, ex // 2, ex % 2
    piece = dp * lax.axis_size("expert") + ex
    mine = piece // 2
    full = 2 * width + LANES
    x_dev, y_dev, core_dev = (dp, (1 - x) * 2 + c), (z * 2 + 1 - y, ex), (dp, x * 2 + 1 - c)
    left, right = pl.ds(0, width), pl.ds(width, width + LANES)
    gather_mid = pl.ds(wide[0], wide[1] - wide[0])
    gather_left, gather_right = pl.ds(0, wide[0]), pl.ds(wide[1], full - wide[1])
    reduce_mid = pl.ds(thin[0], thin[1] - thin[0])
    reduce_left, reduce_right = pl.ds(0, thin[0]), pl.ds(thin[1], full - thin[1])
    packed_right = pl.ds(thin[0], full - thin[1])

    def remote(src, dst, send, recv, device):
        return pltpu.make_async_remote_copy(
            src_ref=src, dst_ref=dst, send_sem=send, recv_sem=recv,
            device_id=device, device_id_type=pl.DeviceIdType.MESH,
        )

    def plane(step):
        reach = jnp.minimum(z, planes - 1 - z)
        away = (step + 1) // 2
        near = jnp.where(step % 2 == 1, z - away, z + away)
        far = jnp.where(z < planes - 1 - z, step, planes - 1 - step)
        return jnp.where(step <= 2 * reach, near, far)

    def z_peer(q):
        return (q * 2 + y, ex)

    own_left = rows.at[z, c, 0, :, left]
    own_right = rows.at[z, c, 0, :, pl.ds(width, width)]
    loads = [
        pltpu.make_async_copy(src, dst, load_sem.at[i])
        for i, (src, dst) in enumerate(
            (
                (ids_hbm, ids_ref), (rw_hbm, rw_ref), (tok_hbm, own_left), (og_hbm, own_right),
                (wg_hbm.at[0], wg_ref), (wu_hbm.at[0], wu_ref), (wd_hbm.at[0], wd_ref),
            )
        )
    ]
    for load in loads:
        load.start()

    barrier = pltpu.get_barrier_semaphore()
    peers = [x_dev, y_dev, core_dev]
    peers += [z_peer((z + d) % planes) for d in range(1, planes)]
    for peer in peers:
        pl.semaphore_signal(barrier, inc=1, device_id=peer, device_id_type=pl.DeviceIdType.MESH)

    loads[0].wait()
    loads[1].wait()
    lane = lax.broadcasted_iota(jnp.int32, (tok_count, LANES), 1)
    ids, weights = ids_ref[...].T, rw_ref[...].T
    table = [jnp.zeros((tok_count, LANES), f32) for _ in range(3)]
    for k in range(ids.shape[1]):
        for part in range(3):
            hit = lane == ids[:, k : k + 1] + part * experts
            table[part] = jnp.where(hit, weights[:, k : k + 1], table[part])
    head = table[0].astype(bf16).astype(f32)
    mid = table[1] - table[1].astype(bf16).astype(f32)
    mid = mid.astype(bf16).astype(f32)
    rest = table[2] - table[2].astype(bf16).astype(f32)
    rest = rest - rest.astype(bf16).astype(f32)
    rows[z, c, 0, :, pl.ds(2 * width, LANES)] = (head + mid + rest).astype(bf16)
    loads[2].wait()
    loads[3].wait()
    pl.semaphore_wait(barrier, len(peers))

    def z_copy(q, way):
        slot = rows.at[q, c, 0]
        return remote(slot, slot, z_ss.at[q, way], z_rs.at[q], z_peer(z + 1 - 2 * way))

    def relay(q, run):
        @pl.when((q <= z) & (z < planes - 1))
        def _():
            run(z_copy(q, 0))

        @pl.when((q >= z) & (z > 0))
        def _():
            run(z_copy(q, 1))

    def x_copy(s, k):
        cols = ((left, right) if s == 0 else (gather_left, gather_right))[k]
        src, dst = rows.at[plane(s), c, 0, :, cols], rows.at[plane(s), c, 1, :, cols]
        return remote(src, dst, x_ss.at[s, k], x_rs.at[s, k], x_dev)

    def y_copy(s, k):
        cols = ((left, right) if s == 0 else (gather_left, gather_right))[k]
        src, dst = rows.at[plane(s), c, 0, :, cols], rows.at[plane(s), c, 2, :, cols]
        return remote(src, dst, y_ss.at[s, k], y_rs.at[s, k], y_dev)

    def xh_copy(s):
        cols = left if s == 0 else gather_left
        src, dst = rows.at[plane(s), c, 2, :, cols], rows.at[plane(s), c, 3, :, cols]
        return remote(src, dst, xh_ss.at[s], xh_rs.at[s], x_dev)

    def yh_copy(s):
        cols = right if s == 0 else gather_right
        src, dst = rows.at[plane(s), c, 1, :, cols], rows.at[plane(s), c, 3, :, cols]
        return remote(src, dst, yh_ss.at[s], yh_rs.at[s], y_dev)

    def wide_slots(q, k):
        return rows.at[q, c, (pl.ds(1, 2), pl.ds(3, 1))[k], :, gather_mid]

    def wide_copy(d, k):
        slots = wide_slots(z, k)
        return remote(slots, slots, wide_ss.at[d - 1, k], wide_rs.at[z, k], z_peer((z + d) % planes))

    def wide_landed(q, k):
        slots = wide_slots(q, k)
        remote(slots, slots, wide_ss.at[0, k], wide_rs.at[q, k], core_dev).wait_recv()

    def core_copy(s, which, core):
        slots, cols = (
            (pl.ds(0, 1), pl.ds(0, full)), (pl.ds(1, 2), gather_left), (pl.ds(1, 2), gather_right),
            (pl.ds(3, 1), gather_left), (pl.ds(3, 1), gather_right), (pl.ds(1, 3), gather_mid),
        )[which]
        ref = rows.at[plane(s), core, slots, :, cols]
        return remote(ref, ref, core_ss.at[s, which], core_rs.at[s, which], core_dev)

    def swap_copy(s, k):
        cols = (left, right)[k]
        src, dst = parts.at[s, 1 - c, :, :, cols], swapped.at[s, :, :, cols]
        return remote(src, dst, swap_ss.at[s, k], swap_rs.at[s, k], core_dev)

    def early_copy(s):
        src = summed.at[s, :, :, reduce_mid]
        return remote(src, early.at[z], early_ss.at[s], early_rs.at[z], z_peer(plane(s)))

    def early_landed(q):
        remote(early.at[q], early.at[q], early_ss.at[0], early_rs.at[q], core_dev).wait_recv()

    def fa_copy(s, own, last):
        cols = left if last else reduce_left
        src, dst = summed.at[s, 1 if own else 3, :, cols], first_a.at[s, own, :, cols]
        return remote(src, dst, fa_ss.at[s, own], fa_rs.at[s, own], x_dev)

    def fb_copy(s, own, last):
        cols = right if last else reduce_right
        at = pl.ds(0, width + LANES) if last else pl.ds(thin[1] - width, full - thin[1])
        src, dst = summed.at[s, 2 if own else 3, :, cols], first_b.at[s, own, :, at]
        return remote(src, dst, fb_ss.at[s, own], fb_rs.at[s, own], y_dev)

    def ta_copy(s, last):
        at = pl.ds(0, width if last else thin[0])
        src, dst = turn_a.at[s, :, at], second_a.at[s, :, at]
        return remote(src, dst, ta_ss.at[s], ta_rs.at[s], y_dev)

    def tb_copy(s, last):
        at = pl.ds(0, width + LANES) if last else pl.ds(thin[1] - width, full - thin[1])
        src, dst = turn_b.at[s, :, at], second_b.at[s, :, at]
        return remote(src, dst, tb_ss.at[s], tb_rs.at[s], x_dev)

    def zo_copy(s):
        return remote(zsend.at[s - 1], zrecv.at[z], zo_ss.at[s - 1], zo_rs.at[z], z_peer(plane(s)))

    def zo_landed(q):
        remote(zrecv.at[q], zrecv.at[q], zo_ss.at[0], zo_rs.at[q], core_dev).wait_recv()

    def gather_one(s):
        q = plane(s)
        if s > 0:
            slot = rows.at[q, c, 0]
            remote(slot, slot, z_ss.at[q, 0], z_rs.at[q], core_dev).wait_recv()
        relay(q, lambda copy: copy.start())
        x_copy(s, 1).start()
        y_copy(s, 0).start()
        x_copy(s, 0).start()
        y_copy(s, 1).start()
        core_copy(s, 0, c).start()

    def gather_two(s):
        y_copy(s, 0).wait_recv()
        xh_copy(s).start()
        x_copy(s, 1).wait_recv()
        yh_copy(s).start()
        x_copy(s, 0).wait_recv()
        core_copy(s, 1, c).start()
        y_copy(s, 1).wait_recv()
        core_copy(s, 2, c).start()

    def gather_three(s):
        xh_copy(s).wait_recv()
        core_copy(s, 3, c).start()
        yh_copy(s).wait_recv()
        core_copy(s, 4, c).start()
        if s > 0:
            wide_landed(plane(s), 0)
            wide_landed(plane(s), 1)
        core_copy(s, 5, c).start()

    def spread(k):
        for d in range(1, planes):
            wide_copy(d, k).start()

    group = 8 * tok_count
    glane = lax.broadcasted_iota(jnp.int32, (group, LANES), 1)

    def compute(s):
        q = plane(s)
        for which in range(6):
            core_copy(s, which, 1 - c).wait_recv()
        x_in = rows[q, :, :, :, 0:width].reshape(group, width)
        g_in = rows[q, :, :, :, width : 2 * width].reshape(group, width)
        gate = contract(x_in, wg_ref[...], 1, 0)
        up = contract(x_in, wu_ref[...], 1, 0)
        back = contract(g_in, wd_ref[...], 1, 1)
        tab = rows[q, :, :, :, 2 * width : full].reshape(group, LANES).astype(f32)
        own = (glane == mine) | (glane == mine + experts) | (glane == mine + 2 * experts)
        weight = jnp.sum(jnp.where(own, tab, 0.0), axis=1, keepdims=True)
        sig = 1.0 / (1.0 + jnp.exp(-gate))
        act = gate * sig
        hidden = act * up
        route = jnp.sum(hidden * back, axis=1, keepdims=True)
        coarse = route.astype(bf16).astype(f32)
        fine = route - coarse
        marks = jnp.where(glane == piece, coarse, jnp.where(glane == piece + LANES // 2, fine, 0.0))
        back = weight * back
        hid = (weight * hidden).astype(bf16)
        gate_pre = (back * up * sig * (1.0 + gate * (1.0 - sig))).astype(bf16)
        up_pre = (back * act).astype(bf16)
        at = pl.ds(pl.multiple_of(q * group, group), group)
        hidden_all[at, :] = hid
        pre_all[at, 0:half] = gate_pre
        pre_all[at, half : 2 * half] = up_pre
        shape = (2, 4, tok_count)
        for n in range(0, width, 2 * tile):
            cols = slice(n, n + 2 * tile)
            out = contract(hid, wd_ref[:, cols], 1, 0)
            parts[s, :, :, :, cols] = out.astype(bf16).reshape(shape + (2 * tile,))
        swap_copy(s, 0).start()
        for n in range(0, width, 2 * tile):
            cols = slice(n, n + 2 * tile)
            grad = contract(gate_pre, wg_ref[cols, :], 1, 1) + contract(up_pre, wu_ref[cols, :], 1, 1)
            after = slice(width + n, width + n + 2 * tile)
            parts[s, :, :, :, after] = grad.astype(bf16).reshape(shape + (2 * tile,))
        parts[s, :, :, :, 2 * width : full] = marks.astype(bf16).reshape(shape + (LANES,))
        swap_copy(s, 1).start()

    def add_cores(s, cols):
        def add(t, carry):
            total = parts[s, c, t, :, cols].astype(f32) + swapped[s, t, :, cols].astype(f32)
            summed[s, t, :, cols] = total.astype(bf16)
            return carry

        lax.fori_loop(0, 4, add, 0)

    def reduce_one(s):
        swap_copy(s, 0).wait_recv()
        add_cores(s, left)
        for own in range(2):
            fa_copy(s, own, False).start()
        swap_copy(s, 1).wait_recv()
        add_cores(s, right)
        for own in range(2):
            fb_copy(s, own, False).start()
        early_copy(s).start()

    def reduce_one_last():
        swap_copy(0, 0).wait_recv()
        add_cores(0, reduce_left)
        swap_copy(0, 1).wait_recv()
        add_cores(0, reduce_right)
        for d in range(1, planes):
            early_landed((z + d) % planes)

        def add(t, carry):
            total = parts[0, c, t, :, reduce_mid].astype(f32) + swapped[0, t, :, reduce_mid].astype(f32)
            for d in range(1, planes):
                total = total + early[(z + d) % planes, t].astype(f32)
            summed[0, t, :, reduce_mid] = total.astype(bf16)
            return carry

        lax.fori_loop(0, 4, add, 0)
        for own in range(2):
            fa_copy(0, own, True).start()
            fb_copy(0, own, True).start()

    def reduce_two(s, last):
        fa_copy(s, 0, last).wait_recv()
        cols = slice(0, width if last else thin[0])
        total = summed[s, 2, :, cols].astype(f32) + first_a[s, 0, :, cols].astype(f32)
        turn_a[s, :, cols] = total.astype(bf16)
        ta_copy(s, last).start()
        fb_copy(s, 0, last).wait_recv()
        begin = width if last else thin[1]
        at = slice(begin - width, full - width)
        total = summed[s, 1, :, begin:full].astype(f32) + first_b[s, 0, :, at].astype(f32)
        turn_b[s, :, at] = total.astype(bf16)
        tb_copy(s, last).start()

    def reduce_three(s, last):
        fa_copy(s, 1, last).wait_recv()
        fb_copy(s, 1, last).wait_recv()
        ta_copy(s, last).wait_recv()
        tb_copy(s, last).wait_recv()
        cols = slice(0, width if last else thin[0])
        begin = width if last else thin[1]
        at = slice(begin - width, full - width)
        total_a = summed[s, 0, :, cols].astype(f32) + first_a[s, 1, :, cols].astype(f32)
        total_a = total_a + second_a[s, :, cols].astype(f32)
        total_b = summed[s, 0, :, begin:full].astype(f32) + first_b[s, 1, :, at].astype(f32)
        total_b = total_b + second_b[s, :, at].astype(f32)
        if last:
            zown[:, 0:width] = total_a
            zown[:, width:full] = total_b
        else:
            zsend[s - 1, :, cols] = total_a.astype(bf16)
            zsend[s - 1, :, packed_right] = total_b.astype(bf16)
            zo_copy(s).start()

    every = planes * group
    tiles = width // tile

    def weight_grads(t, carry):
        cols = pl.ds(pl.multiple_of(t * tile, tile), tile)
        x_in = rows[:, :, :, :, cols].reshape(every, tile)
        after = pl.ds(pl.multiple_of(width + t * tile, tile), tile)
        g_in = rows[:, :, :, :, after].reshape(every, tile)
        both = contract(x_in, pre_all[...], 0, 0).astype(bf16)
        gg_ref[0, cols, :] = both[:, 0:half]
        ug_ref[0, cols, :] = both[:, half : 2 * half]
        dg_ref[0, :, cols] = contract(hidden_all[...], g_in, 0, 0).astype(bf16)
        return carry

    gather_one(0)
    gather_two(0)
    gather_one(1)
    spread(0)
    gather_three(0)
    spread(1)
    gather_one(2)
    gather_two(1)
    for load in loads[4:]:
        load.wait()

    def step(j, carry):
        @pl.when(j < planes)
        def _():
            compute(j)

        @pl.when(j == 0)
        def _():
            for s in range(3, planes):
                gather_one(s)
            gather_two(2)
            gather_three(1)
            for s in range(3, planes):
                gather_two(s)

        for s in range(2, planes):
            @pl.when(j == s - 1)
            def _():
                gather_three(s)

        @pl.when((j >= 2) & (j <= planes))
        def _():
            reduce_two(j - 1, False)

        @pl.when((j >= 3) & (j <= planes + 1))
        def _():
            reduce_three(j - 2, False)

        @pl.when((j >= 1) & (j < planes))
        def _():
            reduce_one(j)

        @pl.when(j == planes)
        def _():
            reduce_one_last()

        @pl.when(j == planes + 1)
        def _():
            reduce_two(0, True)

        @pl.when(j >= planes)
        def _():
            k = j - planes
            lax.fori_loop((k * tiles) // 2, ((k + 1) * tiles) // 2, weight_grads, 0)

        return carry

    lax.fori_loop(0, planes + 2, step, 0)
    reduce_three(0, True)

    total = zown[...]
    total_a, total_m, total_b = total[:, 0 : thin[0]], total[:, thin[0] : thin[1]], total[:, thin[1] : full]
    for d in range(1, planes):
        origin = (z + d) % planes
        zo_landed(origin)
        total_a = total_a + zrecv[origin, :, 0 : thin[0]].astype(f32)
        total_b = total_b + zrecv[origin, :, packed_right].astype(f32)
    lo_ref[:, 0 : thin[0]] = total_a.astype(bf16)
    lo_ref[:, thin[0] : width] = total_m[:, 0 : width - thin[0]].astype(bf16)
    tg_ref[:, 0 : thin[1] - width] = total_m[:, width - thin[0] :].astype(bf16)
    tg_ref[:, thin[1] - width :] = total_b[:, 0 : 2 * width - thin[1]].astype(bf16)
    marks = total_b[:, 2 * width - thin[1] :]
    routes = jnp.zeros((tok_count, LANES), f32)
    for k in range(ids.shape[1]):
        base = 2 * ids[:, k : k + 1]
        hit = (lane == base) | (lane == base + 1)
        hit = hit | (lane == base + LANES // 2) | (lane == base + LANES // 2 + 1)
        value = jnp.sum(jnp.where(hit, marks, 0.0), axis=1, keepdims=True)
        routes = jnp.where(lane == k, value, routes)
    rg_ref[...] = routes.T[0 : ids.shape[1], :]

    for s in range(planes):
        for k in range(2):
            x_copy(s, k).wait_send()
            y_copy(s, k).wait_send()
            swap_copy(s, k).wait_send()
            fa_copy(s, k, s == 0).wait_send()
            fb_copy(s, k, s == 0).wait_send()
        xh_copy(s).wait_send()
        yh_copy(s).wait_send()
        for which in range(6):
            core_copy(s, which, c).wait_send()
        ta_copy(s, s == 0).wait_send()
        tb_copy(s, s == 0).wait_send()
        if s > 0:
            early_copy(s).wait_send()
            zo_copy(s).wait_send()
            for k in range(2):
                wide_copy(s, k).wait_send()
        relay(plane(s), lambda copy: copy.wait_send())


def finish_kernel(
    lo_in, tg_in, rg_in, gg_in, ug_in, dg_in, lo_ref, tg_ref, rg_ref, gg_ref, ug_ref, dg_ref, out_sem, small_sem
):
    copies = []
    for i, (src, dst) in enumerate(((gg_in, gg_ref), (ug_in, ug_ref), (dg_in, dg_ref))):
        count = src.shape[1] // PARTS
        for j in range(PARTS):
            at = pl.ds(j * count, count)
            copies.append(pltpu.make_async_copy(src.at[0, at, :], dst.at[0, at, :], out_sem.at[i, j]))
    for i, (src, dst) in enumerate(((lo_in, lo_ref), (tg_in, tg_ref), (rg_in, rg_ref))):
        copies.append(pltpu.make_async_copy(src, dst, small_sem.at[i]))
    for copy in copies:
        copy.start()
    for copy in copies:
        copy.wait()


def kernel_body(tokens, expert_ids, route_weight, out_grad, gate_weight, up_weight, down_weight):
    dp_size, ex_size = lax.axis_size("dp"), lax.axis_size("expert")
    planes, experts = dp_size // 2, dp_size * ex_size // 2
    tok_count, width = tokens.shape
    half = gate_weight.shape[2]
    tile = TILE
    full = 2 * width + LANES
    wide = (width - WIDE[0], width + WIDE[1])
    thin = (width - THIN[0], width + THIN[1])
    bf16, f32 = jnp.bfloat16, jnp.float32
    every = planes * 8 * tok_count
    dma = pltpu.SemaphoreType.DMA
    vmem = pl.BlockSpec(memory_space=pltpu.VMEM)
    hbm = pl.BlockSpec(memory_space=pltpu.HBM)
    shape = jax.ShapeDtypeStruct
    several = lambda *counts: [dma(counts), dma(counts)]
    sems = [dma((7,)), dma((planes, 2)), dma((planes,))]
    sems += several(planes, 2) * 2 + several(planes) * 2 + [dma((planes - 1, 2)), dma((planes, 2))]
    sems += several(planes, 6) + several(planes, 2) + several(planes) + several(planes, 2) * 2
    sems += several(planes) * 2 + [dma((planes - 1,)), dma((planes,))]
    outs = pl.pallas_call(
        functools.partial(expert_kernel, planes, tok_count, width, half, experts, tile, wide, thin),
        out_shape=(
            pltpu.VMEM(tokens.shape, bf16),
            pltpu.VMEM(tokens.shape, bf16),
            pltpu.VMEM(route_weight.shape[::-1], f32),
            pltpu.VMEM(gate_weight.shape, bf16),
            pltpu.VMEM(up_weight.shape, bf16),
            pltpu.VMEM(down_weight.shape, bf16),
        ),
        in_specs=[hbm] * 7,
        out_specs=[vmem] * 6,
        scratch_shapes=[
            pltpu.VMEM(expert_ids.shape[::-1], jnp.int32),
            pltpu.VMEM(route_weight.shape[::-1], f32),
            pltpu.VMEM((planes, 2, 4, tok_count, full), bf16),
            pltpu.VMEM((planes, 2, 4, tok_count, full), bf16),
            pltpu.VMEM((planes, 4, tok_count, full), bf16),
            pltpu.VMEM((planes, 4, tok_count, full), bf16),
            pltpu.VMEM((planes, 4, tok_count, thin[1] - thin[0]), bf16),
            pltpu.VMEM((planes, 2, tok_count, width), bf16),
            pltpu.VMEM((planes, 2, tok_count, width + LANES), bf16),
            pltpu.VMEM((planes, tok_count, width), bf16),
            pltpu.VMEM((planes, tok_count, width + LANES), bf16),
            pltpu.VMEM((planes, tok_count, width), bf16),
            pltpu.VMEM((planes, tok_count, width + LANES), bf16),
            pltpu.VMEM((planes - 1, tok_count, full - thin[1] + thin[0]), bf16),
            pltpu.VMEM((planes, tok_count, full - thin[1] + thin[0]), bf16),
            pltpu.VMEM((tok_count, full), f32),
            pltpu.VMEM((every, half), bf16),
            pltpu.VMEM((every, 2 * half), bf16),
            pltpu.VMEM(gate_weight.shape[1:], bf16),
            pltpu.VMEM(up_weight.shape[1:], bf16),
            pltpu.VMEM(down_weight.shape[1:], bf16),
        ] + sems,
        compiler_params=pltpu.CompilerParams(
            collective_id=0, has_side_effects=True, vmem_limit_bytes=60620 * 1024
        ),
    )(tokens, expert_ids.T, route_weight.T, out_grad, gate_weight, up_weight, down_weight)
    lo, tg, rg, gg, ug, dg = pl.pallas_call(
        finish_kernel,
        out_shape=tuple(shape(o.shape, o.dtype) for o in outs),
        in_specs=[vmem] * 6,
        out_specs=[hbm] * 6,
        scratch_shapes=[dma((3, PARTS)), dma((3,))],
        compiler_params=pltpu.CompilerParams(vmem_limit_bytes=4 * 1024 * 1024),
    )(*outs)
    return lo, tg, rg.T, gg, ug, dg


def solution(mesh):
    in_specs = (
        P(("dp", "expert"), None),
        P(("dp", "expert"), None),
        P(("dp", "expert"), None),
        P(("dp", "expert"), None),
        P(("dp", "expert"), None, None),
        P(("dp", "expert"), None, None),
        P(("dp", "expert"), None, None),
    )
    out_specs = (
        P(("dp", "expert"), None),
        P(("dp", "expert"), None),
        P(("dp", "expert"), None),
        P(("dp", "expert"), None, None),
        P(("dp", "expert"), None, None),
        P(("dp", "expert"), None, None),
    )
    dp_size, ex_size = mesh.shape["dp"], mesh.shape["expert"]
    pieces = dp_size * ex_size

    def step(tokens, expert_ids, *rest):
        capacity = 2 * (tokens.shape[0] * expert_ids.shape[1] // (pieces // 2))
        fits = ex_size == 4 and dp_size >= 4 and dp_size % 2 == 0 and 3 * pieces // 2 <= LANES
        fits = fits and pieces <= LANES // 2 and tokens.shape[1] % (2 * TILE) == 0
        fits = fits and tokens.shape[1] > max(WIDE + THIN)
        form = kernel_body if fits and capacity >= tokens.shape[0] else body
        return form(tokens, expert_ids, *rest)

    return jax.shard_map(step, mesh=mesh, in_specs=in_specs, out_specs=out_specs, check_vma=False)
```

```python
import functools

import jax
import jax.numpy as jnp
from jax import lax
from jax.experimental import pallas as pl
from jax.experimental.pallas import tpu as pltpu
from jax.sharding import PartitionSpec as P

LANES = 128
TILE = 256
PARTS = 4
WIDE = (256, 256)
WIDE_STEPS = (1, 2, 3)
THIN = (512, 512)
EARLY_STEPS = (1, 2)


def from_partner(shard, axis, apart):
    return lax.ppermute(shard, axis, [(i, i ^ 1 << apart) for i in range(lax.axis_size(axis))])


def contract(left_op, right_op, left_dim, right_dim):
    return lax.dot_general(
        left_op,
        right_op,
        (((left_dim,), (right_dim,)), ((), ())),
        preferred_element_type=jnp.float32,
    )


def deliver(buffer, dp_size, ex_size, experts, capacity, backward):
    feat_width = buffer.shape[1]
    doubled = jnp.broadcast_to(
        buffer.reshape(experts, 1, capacity, feat_width), (experts, 2, capacity, feat_width)
    )
    doubled = doubled.reshape(dp_size, ex_size, capacity, feat_width)
    if backward:
        arrived = lax.all_to_all(
            lax.all_to_all(doubled, "dp", split_axis=0, concat_axis=0, tiled=True),
            "expert",
            split_axis=1,
            concat_axis=1,
            tiled=True,
        )
    else:
        arrived = lax.all_to_all(
            lax.all_to_all(doubled, "dp", split_axis=0, concat_axis=0, tiled=True),
            "expert",
            split_axis=1,
            concat_axis=1,
            tiled=True,
        )
    return arrived.reshape(-1, feat_width)


def bring_back(partials_in, dp_size, ex_size, experts, capacity, half_index, backward):
    feat_width = partials_in.shape[1]
    if backward:
        partner = from_partner(partials_in, "expert", 0)
    else:
        partner = from_partner(partials_in, "expert", 0)
    summed = (partials_in.astype(jnp.float32) + partner.astype(jnp.float32)).astype(jnp.bfloat16)
    summed = summed.reshape(dp_size, ex_size, capacity, feat_width)
    own_half = lax.dynamic_slice_in_dim(summed, half_index * (capacity // 2), capacity // 2, 2)
    if backward:
        returned = lax.all_to_all(
            lax.all_to_all(own_half, "dp", split_axis=0, concat_axis=0, tiled=True),
            "expert",
            split_axis=1,
            concat_axis=1,
            tiled=True,
        )
    else:
        returned = lax.all_to_all(
            lax.all_to_all(own_half, "dp", split_axis=0, concat_axis=0, tiled=True),
            "expert",
            split_axis=1,
            concat_axis=1,
            tiled=True,
        )
    merged = returned.reshape(experts, capacity, feat_width)
    return merged.reshape(experts * capacity, feat_width)


def body(tokens, expert_ids, route_weight, out_grad, gate_weight, up_weight, down_weight):
    dp_size = lax.axis_size("dp")
    ex_size = lax.axis_size("expert")
    tok_count, feat_width = tokens.shape
    top_count = expert_ids.shape[1]
    experts = dp_size * ex_size // 2
    assigned = tok_count * top_count
    capacity = 2 * (assigned // experts)
    half_index = lax.axis_index("expert") % 2
    flat_ids = expert_ids.reshape(-1)
    order = jnp.arange(assigned, dtype=jnp.int32)
    earlier = (flat_ids[:, None] == flat_ids[None, :]) & (order[None, :] < order[:, None])
    slot_ids = jnp.sum(earlier.astype(jnp.int32), axis=1)
    place_row = flat_ids * capacity + slot_ids
    source = (
        jnp.full((experts * capacity,), -1, jnp.int32)
        .at[place_row]
        .set(jnp.arange(assigned, dtype=jnp.int32))
    )
    filled = source >= 0
    assign = jnp.maximum(source, 0)
    rows_tok = assign // top_count
    send_rows = jnp.where(filled[:, None], tokens[rows_tok], jnp.zeros((), jnp.bfloat16))
    in_rows = deliver(send_rows, dp_size, ex_size, experts, capacity, False)
    w_gate = gate_weight[0]
    w_up = up_weight[0]
    w_down = down_weight[0]
    gate_act = jnp.dot(in_rows, w_gate, preferred_element_type=jnp.float32)
    up_act = jnp.dot(in_rows, w_up, preferred_element_type=jnp.float32)
    sig_gate = jax.nn.sigmoid(gate_act)
    hidden = (gate_act * sig_gate * up_act).astype(jnp.bfloat16)
    partial_value = jnp.dot(hidden, w_down, preferred_element_type=jnp.float32).astype(jnp.bfloat16)
    expert_table = bring_back(partial_value, dp_size, ex_size, experts, capacity, half_index, False)
    expert_rows = expert_table[place_row].reshape(tok_count, top_count, feat_width)
    layer_out = jnp.sum(route_weight[:, :, None] * expert_rows.astype(jnp.float32), axis=1).astype(
        jnp.bfloat16
    )
    route_grad = jnp.einsum("tkd,td->tk", expert_rows, out_grad, preferred_element_type=jnp.float32)
    scaled = (route_weight[:, :, None] * out_grad[:, None, :].astype(jnp.float32)).astype(
        jnp.bfloat16
    )
    scaled = scaled.reshape(assigned, feat_width)
    send_grad = jnp.where(filled[:, None], scaled[assign], jnp.zeros((), jnp.bfloat16))
    grad_rows = deliver(send_grad, dp_size, ex_size, experts, capacity, True)
    hidden_grad = contract(grad_rows, w_down, 1, 1)
    gate_pre = (hidden_grad * up_act * sig_gate * (1.0 + gate_act * (1.0 - sig_gate))).astype(
        jnp.bfloat16
    )
    up_pre = (hidden_grad * gate_act * sig_gate).astype(jnp.bfloat16)
    partial_grad = (contract(gate_pre, w_gate, 1, 1) + contract(up_pre, w_up, 1, 1)).astype(
        jnp.bfloat16
    )
    gate_grad = contract(in_rows, gate_pre, 0, 0).astype(jnp.bfloat16)
    up_grad = contract(in_rows, up_pre, 0, 0).astype(jnp.bfloat16)
    down_grad = contract(hidden, grad_rows, 0, 0).astype(jnp.bfloat16)
    grad_table = bring_back(partial_grad, dp_size, ex_size, experts, capacity, half_index, True)
    expert_grad = grad_table[place_row].reshape(tok_count, top_count, feat_width)
    token_grad = jnp.sum(expert_grad.astype(jnp.float32), axis=1).astype(jnp.bfloat16)
    return (layer_out, token_grad, route_grad, gate_grad[None], up_grad[None], down_grad[None])


def expert_kernel(
    planes, tok_count, width, half, experts, tile, wide, thin,
    tok_hbm, ids_hbm, rw_hbm, og_hbm, wg_hbm, wu_hbm, wd_hbm,
    lo_ref, tg_ref, rg_ref, gg_ref, ug_ref, dg_ref,
    ids_ref, rw_ref, rows, parts, swapped, summed, early, first_a, first_b, turn_a, turn_b, second_a, second_b,
    zsend, zrecv, zown, hidden_all, pre_all, wg_ref, wu_ref, wd_ref,
    load_sem, z_ss, z_rs, x_ss, x_rs, y_ss, y_rs, xh_ss, xh_rs, yh_ss, yh_rs, wide_ss, wide_rs,
    core_ss, core_rs, swap_ss, swap_rs, early_ss, early_rs, fa_ss, fa_rs, fb_ss, fb_rs,
    ta_ss, ta_rs, tb_ss, tb_rs, zo_ss, zo_rs,
):
    f32, bf16 = jnp.float32, jnp.bfloat16
    dp, ex = lax.axis_index("dp"), lax.axis_index("expert")
    z, y, x, c = dp // 2, dp % 2, ex // 2, ex % 2
    piece = dp * lax.axis_size("expert") + ex
    mine = piece // 2
    full = 2 * width + LANES
    x_dev, y_dev, core_dev = (dp, (1 - x) * 2 + c), (z * 2 + 1 - y, ex), (dp, x * 2 + 1 - c)
    left, right = pl.ds(0, width), pl.ds(width, width + LANES)
    gather_mid = pl.ds(wide[0], wide[1] - wide[0])
    gather_left, gather_right = pl.ds(0, wide[0]), pl.ds(wide[1], full - wide[1])
    reduce_mid = pl.ds(thin[0], thin[1] - thin[0])
    reduce_left, reduce_right = pl.ds(0, thin[0]), pl.ds(thin[1], full - thin[1])
    packed_right = pl.ds(thin[0], full - thin[1])

    def remote(src, dst, send, recv, device):
        return pltpu.make_async_remote_copy(
            src_ref=src, dst_ref=dst, send_sem=send, recv_sem=recv,
            device_id=device, device_id_type=pl.DeviceIdType.MESH,
        )

    def plane(step):
        return z ^ step

    def z_peer(q):
        return (q * 2 + y, ex)

    own_left = rows.at[z, c, 0, :, left]
    own_right = rows.at[z, c, 0, :, pl.ds(width, width)]
    loads = [
        pltpu.make_async_copy(src, dst, load_sem.at[i])
        for i, (src, dst) in enumerate(
            (
                (ids_hbm, ids_ref), (rw_hbm, rw_ref), (tok_hbm, own_left), (og_hbm, own_right),
                (wg_hbm.at[0], wg_ref), (wu_hbm.at[0], wu_ref), (wd_hbm.at[0], wd_ref),
            )
        )
    ]
    for load in loads:
        load.start()

    barrier = pltpu.get_barrier_semaphore()
    peers = [x_dev, y_dev, core_dev]
    peers += [z_peer((z + d) % planes) for d in range(1, planes)]
    for peer in peers:
        pl.semaphore_signal(barrier, inc=1, device_id=peer, device_id_type=pl.DeviceIdType.MESH)

    loads[0].wait()
    loads[1].wait()
    lane = lax.broadcasted_iota(jnp.int32, (tok_count, LANES), 1)
    ids, weights = ids_ref[...].T, rw_ref[...].T
    table = [jnp.zeros((tok_count, LANES), f32) for _ in range(3)]
    for k in range(ids.shape[1]):
        for part in range(3):
            hit = lane == ids[:, k : k + 1] + part * experts
            table[part] = jnp.where(hit, weights[:, k : k + 1], table[part])
    head = table[0].astype(bf16).astype(f32)
    mid = table[1] - table[1].astype(bf16).astype(f32)
    mid = mid.astype(bf16).astype(f32)
    rest = table[2] - table[2].astype(bf16).astype(f32)
    rest = rest - rest.astype(bf16).astype(f32)
    rows[z, c, 0, :, pl.ds(2 * width, LANES)] = (head + mid + rest).astype(bf16)
    loads[2].wait()
    loads[3].wait()
    pl.semaphore_wait(barrier, len(peers))

    def z_copy(q, way, k):
        part = rows.at[q, c, 0, :, (left, right)[k]]
        return remote(part, part, z_ss.at[q, way, k], z_rs.at[q, k], z_peer(z + 1 - 2 * way))

    def relay(q, k, run):
        @pl.when((q <= z) & (z < planes - 1))
        def _():
            run(z_copy(q, 0, k))

        @pl.when((q >= z) & (z > 0))
        def _():
            run(z_copy(q, 1, k))

    def z_landed(q, k):
        part = rows.at[q, c, 0, :, (left, right)[k]]
        remote(part, part, z_ss.at[q, 0, k], z_rs.at[q, k], core_dev).wait_recv()

    def along(away, k):
        @pl.when(z >= away)
        def _():
            z_landed(z - away, k)
            relay(z - away, k, lambda copy: copy.start())

        @pl.when(z < planes - away)
        def _():
            z_landed(z + away, k)
            relay(z + away, k, lambda copy: copy.start())

    def gather_cols(s, k):
        return ((gather_left, gather_right) if s in WIDE_STEPS else (left, right))[k]

    def x_copy(s, k):
        cols = gather_cols(s, k)
        src, dst = rows.at[plane(s), c, 0, :, cols], rows.at[plane(s), c, 1, :, cols]
        return remote(src, dst, x_ss.at[s, k], x_rs.at[s, k], x_dev)

    def y_copy(s, k):
        cols = gather_cols(s, k)
        src, dst = rows.at[plane(s), c, 0, :, cols], rows.at[plane(s), c, 2, :, cols]
        return remote(src, dst, y_ss.at[s, k], y_rs.at[s, k], y_dev)

    def xh_copy(s):
        cols = gather_cols(s, 0)
        src, dst = rows.at[plane(s), c, 2, :, cols], rows.at[plane(s), c, 3, :, cols]
        return remote(src, dst, xh_ss.at[s], xh_rs.at[s], x_dev)

    def yh_copy(s):
        cols = gather_cols(s, 1)
        src, dst = rows.at[plane(s), c, 1, :, cols], rows.at[plane(s), c, 3, :, cols]
        return remote(src, dst, yh_ss.at[s], yh_rs.at[s], y_dev)

    def wide_slots(q, k):
        return rows.at[q, c, (pl.ds(1, 2), pl.ds(3, 1))[k], :, gather_mid]

    def wide_copy(s, k):
        slots = wide_slots(z, k)
        return remote(slots, slots, wide_ss.at[s - 1, k], wide_rs.at[z, k], z_peer(plane(s)))

    def wide_landed(q, k):
        slots = wide_slots(q, k)
        remote(slots, slots, wide_ss.at[0, k], wide_rs.at[q, k], core_dev).wait_recv()

    def core_copy(s, which, core):
        slots, cols = (
            (pl.ds(0, 1), pl.ds(0, full)), (pl.ds(1, 2), gather_left), (pl.ds(1, 2), gather_right),
            (pl.ds(3, 1), gather_left), (pl.ds(3, 1), gather_right), (pl.ds(1, 3), gather_mid),
        )[which]
        ref = rows.at[plane(s), core, slots, :, cols]
        return remote(ref, ref, core_ss.at[s, which], core_rs.at[s, which], core_dev)

    def whole(s):
        return s not in EARLY_STEPS

    def swap_copy(s, k):
        cols = (left, right)[k]
        src, dst = parts.at[s, 1 - c, :, :, cols], swapped.at[s, :, :, cols]
        return remote(src, dst, swap_ss.at[s, k], swap_rs.at[s, k], core_dev)

    def early_copy(s):
        src = summed.at[s, :, :, reduce_mid]
        return remote(src, early.at[z], early_ss.at[s], early_rs.at[z], z_peer(plane(s)))

    def early_landed(q):
        remote(early.at[q], early.at[q], early_ss.at[0], early_rs.at[q], core_dev).wait_recv()

    def fa_copy(s, own):
        last = whole(s)
        cols = left if last else reduce_left
        src, dst = summed.at[s, 1 if own else 3, :, cols], first_a.at[s, own, :, cols]
        return remote(src, dst, fa_ss.at[s, own], fa_rs.at[s, own], x_dev)

    def fb_copy(s, own):
        last = whole(s)
        cols = right if last else reduce_right
        at = pl.ds(0, width + LANES) if last else pl.ds(thin[1] - width, full - thin[1])
        src, dst = summed.at[s, 2 if own else 3, :, cols], first_b.at[s, own, :, at]
        return remote(src, dst, fb_ss.at[s, own], fb_rs.at[s, own], y_dev)

    def ta_copy(s):
        last = whole(s)
        at = pl.ds(0, width if last else thin[0])
        src, dst = turn_a.at[s, :, at], second_a.at[s, :, at]
        return remote(src, dst, ta_ss.at[s], ta_rs.at[s], y_dev)

    def tb_copy(s):
        last = whole(s)
        at = pl.ds(0, width + LANES) if last else pl.ds(thin[1] - width, full - thin[1])
        src, dst = turn_b.at[s, :, at], second_b.at[s, :, at]
        return remote(src, dst, tb_ss.at[s], tb_rs.at[s], x_dev)

    def zo_cols(s, k):
        if whole(s):
            return (left, right)[k]
        return (pl.ds(0, thin[0]), packed_right)[k]

    def zo_copy(s, k):
        cols = zo_cols(s, k)
        src, dst = zsend.at[s - 1, :, cols], zrecv.at[s - 1, :, cols]
        return remote(src, dst, zo_ss.at[s - 1, k], zo_rs.at[s - 1, k], z_peer(plane(s)))

    def begin():
        relay(z, 0, lambda copy: copy.start())
        x_copy(0, 1).start()
        y_copy(0, 0).start()
        relay(z, 1, lambda copy: copy.start())
        x_copy(0, 0).start()
        y_copy(0, 1).start()
        core_copy(0, 0, c).start()

    def pass_on(s, k):
        x_copy(s, k).start()
        y_copy(s, k).start()
        if k == 1:
            core_copy(s, 0, c).start()

    def across_x(s):
        y_copy(s, 0).wait_recv()
        xh_copy(s).start()

    def across_y(s):
        x_copy(s, 1).wait_recv()
        yh_copy(s).start()

    def to_core(s):
        x_copy(s, 0).wait_recv()
        core_copy(s, 1, c).start()
        y_copy(s, 1).wait_recv()
        core_copy(s, 2, c).start()

    def gathered(s):
        xh_copy(s).wait_recv()
        core_copy(s, 3, c).start()
        yh_copy(s).wait_recv()
        core_copy(s, 4, c).start()
        if s in WIDE_STEPS:
            wide_landed(plane(s), 0)
            wide_landed(plane(s), 1)
        core_copy(s, 5, c).start()

    def spread(k):
        for s in WIDE_STEPS:
            wide_copy(s, k).start()

    group = 8 * tok_count
    glane = lax.broadcasted_iota(jnp.int32, (group, LANES), 1)

    def group_at(s):
        return pl.ds(pl.multiple_of(plane(s) * group, group), group)

    def forward(s):
        q = plane(s)
        for which in range(6):
            core_copy(s, which, 1 - c).wait_recv()
        x_in = rows[q, :, :, :, 0:width].reshape(group, width)
        g_in = rows[q, :, :, :, width : 2 * width].reshape(group, width)
        gate = contract(x_in, wg_ref[...], 1, 0)
        up = contract(x_in, wu_ref[...], 1, 0)
        back = contract(g_in, wd_ref[...], 1, 1)
        tab = rows[q, :, :, :, 2 * width : full].reshape(group, LANES).astype(f32)
        own = (glane == mine) | (glane == mine + experts) | (glane == mine + 2 * experts)
        weight = jnp.sum(jnp.where(own, tab, 0.0), axis=1, keepdims=True)
        sig = 1.0 / (1.0 + jnp.exp(-gate))
        act = gate * sig
        hidden = act * up
        route = jnp.sum(hidden * back, axis=1, keepdims=True)
        coarse = route.astype(bf16).astype(f32)
        fine = route - coarse
        marks = jnp.where(glane == piece, coarse, jnp.where(glane == piece + LANES // 2, fine, 0.0))
        parts[s, :, :, :, 2 * width : full] = marks.astype(bf16).reshape(2, 4, tok_count, LANES)
        back = weight * back
        hidden_all[group_at(s), :] = (weight * hidden).astype(bf16)
        pre_all[group_at(s), 0:half] = (back * up * sig * (1.0 + gate * (1.0 - sig))).astype(bf16)
        pre_all[group_at(s), half : 2 * half] = (back * act).astype(bf16)

    def outward(s):
        hid = hidden_all[group_at(s), :]
        for n in range(0, width, 2 * tile):
            cols = slice(n, n + 2 * tile)
            out = contract(hid, wd_ref[:, cols], 1, 0)
            parts[s, :, :, :, cols] = out.astype(bf16).reshape(2, 4, tok_count, 2 * tile)
        swap_copy(s, 0).start()

    def inward(s):
        gate_pre, up_pre = pre_all[group_at(s), 0:half], pre_all[group_at(s), half : 2 * half]
        for n in range(0, width, 2 * tile):
            cols = slice(n, n + 2 * tile)
            grad = contract(gate_pre, wg_ref[cols, :], 1, 1) + contract(up_pre, wu_ref[cols, :], 1, 1)
            after = slice(width + n, width + n + 2 * tile)
            parts[s, :, :, :, after] = grad.astype(bf16).reshape(2, 4, tok_count, 2 * tile)
        swap_copy(s, 1).start()

    def add_cores(s, cols):
        def add(t, carry):
            total = parts[s, c, t, :, cols].astype(f32) + swapped[s, t, :, cols].astype(f32)
            summed[s, t, :, cols] = total.astype(bf16)
            return carry

        lax.fori_loop(0, 4, add, 0)

    def reduce_left_half(s):
        swap_copy(s, 0).wait_recv()
        add_cores(s, left)
        for own in range(2):
            fa_copy(s, own).start()

    def reduce_right_half(s):
        swap_copy(s, 1).wait_recv()
        add_cores(s, right)
        for own in range(2):
            fb_copy(s, own).start()
        if s in EARLY_STEPS:
            early_copy(s).start()

    def add_own():
        swap_copy(0, 0).wait_recv()
        add_cores(0, reduce_left)
        swap_copy(0, 1).wait_recv()
        add_cores(0, reduce_right)

    def reduce_own():
        for s in EARLY_STEPS:
            early_landed(plane(s))

        def add(t, carry):
            total = parts[0, c, t, :, reduce_mid].astype(f32) + swapped[0, t, :, reduce_mid].astype(f32)
            for s in EARLY_STEPS:
                total = total + early[plane(s), t].astype(f32)
            summed[0, t, :, reduce_mid] = total.astype(bf16)
            return carry

        lax.fori_loop(0, 4, add, 0)
        for own in range(2):
            fa_copy(0, own).start()
            fb_copy(0, own).start()

    def turn_left(s):
        last = whole(s)
        fa_copy(s, 0).wait_recv()
        cols = slice(0, width if last else thin[0])
        total = summed[s, 2, :, cols].astype(f32) + first_a[s, 0, :, cols].astype(f32)
        turn_a[s, :, cols] = total.astype(bf16)
        ta_copy(s).start()

    def turn_right(s):
        last = whole(s)
        fb_copy(s, 0).wait_recv()
        begin = width if last else thin[1]
        at = slice(begin - width, full - width)
        total = summed[s, 1, :, begin:full].astype(f32) + first_b[s, 0, :, at].astype(f32)
        turn_b[s, :, at] = total.astype(bf16)
        tb_copy(s).start()

    def collect_left(s):
        fa_copy(s, 1).wait_recv()
        ta_copy(s).wait_recv()
        cols = slice(0, width if whole(s) else thin[0])
        total = summed[s, 0, :, cols].astype(f32) + first_a[s, 1, :, cols].astype(f32)
        total = total + second_a[s, :, cols].astype(f32)
        if s == 0:
            zown[:, cols] = total
        else:
            zsend[s - 1, :, cols] = total.astype(bf16)
            zo_copy(s, 0).start()

    def collect_right(s):
        fb_copy(s, 1).wait_recv()
        tb_copy(s).wait_recv()
        begin = width if whole(s) else thin[1]
        at = slice(begin - width, full - width)
        total = summed[s, 0, :, begin:full].astype(f32) + first_b[s, 1, :, at].astype(f32)
        total = total + second_b[s, :, at].astype(f32)
        if s == 0:
            zown[:, width:full] = total
        else:
            zsend[s - 1, :, zo_cols(s, 1)] = total.astype(bf16)
            zo_copy(s, 1).start()

    every = planes * group
    tiles = width // tile

    def weight_tile(t, carry):
        cols = pl.ds(pl.multiple_of(t * tile, tile), tile)
        x_in = rows[:, :, :, :, cols].reshape(every, tile)
        after = pl.ds(pl.multiple_of(width + t * tile, tile), tile)
        g_in = rows[:, :, :, :, after].reshape(every, tile)
        both = contract(x_in, pre_all[...], 0, 0).astype(bf16)
        gg_ref[0, cols, :] = both[:, 0:half]
        ug_ref[0, cols, :] = both[:, half : 2 * half]
        dg_ref[0, :, cols] = contract(hidden_all[...], g_in, 0, 0).astype(bf16)
        return carry

    def weights_ready():
        for load in loads[4:]:
            load.wait()

    def weight_grads(first, last):
        lax.fori_loop(first * tiles // 8, last * tiles // 8, weight_tile, 0)

    begin()
    along(1, 0)
    pass_on(1, 0)
    across_y(0)
    across_x(0)
    along(1, 1)
    pass_on(1, 1)
    along(2, 0)
    to_core(0)
    pass_on(2, 0)
    gathered(0)
    along(2, 1)
    pass_on(2, 1)
    weights_ready()
    spread(0)
    across_y(1)
    across_x(1)
    forward(0)
    spread(1)
    across_x(2)
    along(3, 0)
    pass_on(3, 0)
    across_y(2)
    to_core(2)
    to_core(1)
    gathered(1)
    along(3, 1)
    pass_on(3, 1)
    forward(1)
    outward(1)
    gathered(2)
    across_x(3)
    inward(1)
    across_y(3)
    reduce_left_half(1)
    forward(2)
    outward(2)
    to_core(3)
    reduce_right_half(1)
    inward(2)
    reduce_left_half(2)
    gathered(3)
    inward(0)
    reduce_right_half(2)
    forward(3)
    turn_right(1)
    inward(3)
    turn_left(2)
    outward(3)
    turn_right(2)
    reduce_right_half(3)
    reduce_left_half(3)
    outward(0)
    collect_left(2)
    add_own()
    turn_right(3)
    collect_right(2)
    turn_left(1)
    turn_left(3)
    weight_grads(0, 2)
    collect_right(1)
    reduce_own()
    collect_right(3)
    collect_left(1)
    collect_left(3)
    weight_grads(4, 6)
    turn_right(0)
    turn_left(0)
    weight_grads(6, 8)
    weight_grads(2, 4)
    collect_left(0)
    collect_right(0)
    total_a, total_b = zown[:, 0:width], zown[:, width:full]
    ends = (width - thin[0], thin[1] - width)
    for s in range(1, planes):
        zo_copy(s, 0).wait_recv()
        zo_copy(s, 1).wait_recv()
        more_a, more_b = (zrecv[s - 1, :, zo_cols(s, k)].astype(f32) for k in range(2))
        if not whole(s):
            more_a = jnp.concatenate([more_a, jnp.zeros((tok_count, ends[0]), f32)], axis=1)
            more_b = jnp.concatenate([jnp.zeros((tok_count, ends[1]), f32), more_b], axis=1)
        total_a, total_b = total_a + more_a, total_b + more_b
    lo_ref[...] = total_a.astype(bf16)
    tg_ref[...] = total_b[:, 0:width].astype(bf16)
    marks = total_b[:, width:]
    routes = jnp.zeros((tok_count, LANES), f32)
    for k in range(ids.shape[1]):
        base = 2 * ids[:, k : k + 1]
        hit = (lane == base) | (lane == base + 1)
        hit = hit | (lane == base + LANES // 2) | (lane == base + LANES // 2 + 1)
        value = jnp.sum(jnp.where(hit, marks, 0.0), axis=1, keepdims=True)
        routes = jnp.where(lane == k, value, routes)
    rg_ref[...] = routes.T[0 : ids.shape[1], :]

    for s in range(planes):
        for k in range(2):
            x_copy(s, k).wait_send()
            y_copy(s, k).wait_send()
            swap_copy(s, k).wait_send()
            fa_copy(s, k).wait_send()
            fb_copy(s, k).wait_send()
            relay(plane(s), k, lambda copy: copy.wait_send())
            if s > 0:
                zo_copy(s, k).wait_send()
            if s in WIDE_STEPS:
                wide_copy(s, k).wait_send()
        if s in EARLY_STEPS:
            early_copy(s).wait_send()
        xh_copy(s).wait_send()
        yh_copy(s).wait_send()
        for which in range(6):
            core_copy(s, which, c).wait_send()
        ta_copy(s).wait_send()
        tb_copy(s).wait_send()


def finish_kernel(
    lo_in, tg_in, rg_in, gg_in, ug_in, dg_in, lo_ref, tg_ref, rg_ref, gg_ref, ug_ref, dg_ref, out_sem, small_sem
):
    copies = []
    for i, (src, dst) in enumerate(((gg_in, gg_ref), (ug_in, ug_ref), (dg_in, dg_ref))):
        count = src.shape[1] // PARTS
        for j in range(PARTS):
            at = pl.ds(j * count, count)
            copies.append(pltpu.make_async_copy(src.at[0, at, :], dst.at[0, at, :], out_sem.at[i, j]))
    for i, (src, dst) in enumerate(((lo_in, lo_ref), (tg_in, tg_ref), (rg_in, rg_ref))):
        copies.append(pltpu.make_async_copy(src, dst, small_sem.at[i]))
    for copy in copies:
        copy.start()
    for copy in copies:
        copy.wait()


def kernel_body(tokens, expert_ids, route_weight, out_grad, gate_weight, up_weight, down_weight):
    dp_size, ex_size = lax.axis_size("dp"), lax.axis_size("expert")
    planes, experts = dp_size // 2, dp_size * ex_size // 2
    tok_count, width = tokens.shape
    half = gate_weight.shape[2]
    tile = TILE
    full = 2 * width + LANES
    wide = (width - WIDE[0], width + WIDE[1])
    thin = (width - THIN[0], width + THIN[1])
    bf16, f32 = jnp.bfloat16, jnp.float32
    every = planes * 8 * tok_count
    dma = pltpu.SemaphoreType.DMA
    vmem = pl.BlockSpec(memory_space=pltpu.VMEM)
    hbm = pl.BlockSpec(memory_space=pltpu.HBM)
    shape = jax.ShapeDtypeStruct
    several = lambda *counts: [dma(counts), dma(counts)]
    sems = [dma((7,)), dma((planes, 2, 2)), dma((planes, 2))]
    sems += several(planes, 2) * 2 + several(planes) * 2 + [dma((planes - 1, 2)), dma((planes, 2))]
    sems += several(planes, 6) + several(planes, 2) + several(planes) + several(planes, 2) * 2
    sems += several(planes) * 2 + several(planes - 1, 2)
    outs = pl.pallas_call(
        functools.partial(expert_kernel, planes, tok_count, width, half, experts, tile, wide, thin),
        out_shape=(
            pltpu.VMEM(tokens.shape, bf16),
            pltpu.VMEM(tokens.shape, bf16),
            pltpu.VMEM(route_weight.shape[::-1], f32),
            pltpu.VMEM(gate_weight.shape, bf16),
            pltpu.VMEM(up_weight.shape, bf16),
            pltpu.VMEM(down_weight.shape, bf16),
        ),
        in_specs=[hbm] * 7,
        out_specs=[vmem] * 6,
        scratch_shapes=[
            pltpu.VMEM(expert_ids.shape[::-1], jnp.int32),
            pltpu.VMEM(route_weight.shape[::-1], f32),
            pltpu.VMEM((planes, 2, 4, tok_count, full), bf16),
            pltpu.VMEM((planes, 2, 4, tok_count, full), bf16),
            pltpu.VMEM((planes, 4, tok_count, full), bf16),
            pltpu.VMEM((planes, 4, tok_count, full), bf16),
            pltpu.VMEM((planes, 4, tok_count, thin[1] - thin[0]), bf16),
            pltpu.VMEM((planes, 2, tok_count, width), bf16),
            pltpu.VMEM((planes, 2, tok_count, width + LANES), bf16),
            pltpu.VMEM((planes, tok_count, width), bf16),
            pltpu.VMEM((planes, tok_count, width + LANES), bf16),
            pltpu.VMEM((planes, tok_count, width), bf16),
            pltpu.VMEM((planes, tok_count, width + LANES), bf16),
            pltpu.VMEM((planes - 1, tok_count, full), bf16),
            pltpu.VMEM((planes - 1, tok_count, full), bf16),
            pltpu.VMEM((tok_count, full), f32),
            pltpu.VMEM((every, half), bf16),
            pltpu.VMEM((every, 2 * half), bf16),
            pltpu.VMEM(gate_weight.shape[1:], bf16),
            pltpu.VMEM(up_weight.shape[1:], bf16),
            pltpu.VMEM(down_weight.shape[1:], bf16),
        ] + sems,
        compiler_params=pltpu.CompilerParams(
            collective_id=0, has_side_effects=True, vmem_limit_bytes=60620 * 1024
        ),
    )(tokens, expert_ids.T, route_weight.T, out_grad, gate_weight, up_weight, down_weight)
    lo, tg, rg, gg, ug, dg = pl.pallas_call(
        finish_kernel,
        out_shape=tuple(shape(o.shape, o.dtype) for o in outs),
        in_specs=[vmem] * 6,
        out_specs=[hbm] * 6,
        scratch_shapes=[dma((3, PARTS)), dma((3,))],
        compiler_params=pltpu.CompilerParams(vmem_limit_bytes=4 * 1024 * 1024),
    )(*outs)
    return lo, tg, rg.T, gg, ug, dg


def solution(mesh):
    in_specs = (
        P(("dp", "expert"), None),
        P(("dp", "expert"), None),
        P(("dp", "expert"), None),
        P(("dp", "expert"), None),
        P(("dp", "expert"), None, None),
        P(("dp", "expert"), None, None),
        P(("dp", "expert"), None, None),
    )
    out_specs = (
        P(("dp", "expert"), None),
        P(("dp", "expert"), None),
        P(("dp", "expert"), None),
        P(("dp", "expert"), None, None),
        P(("dp", "expert"), None, None),
        P(("dp", "expert"), None, None),
    )
    dp_size, ex_size = mesh.shape["dp"], mesh.shape["expert"]
    pieces = dp_size * ex_size

    def step(tokens, expert_ids, *rest):
        capacity = 2 * (tokens.shape[0] * expert_ids.shape[1] // (pieces // 2))
        fits = ex_size == 4 and dp_size == 8 and 3 * pieces // 2 <= LANES
        fits = fits and pieces <= LANES // 2 and tokens.shape[1] % (2 * TILE) == 0
        fits = fits and tokens.shape[1] > max(WIDE + THIN)
        form = kernel_body if fits and capacity >= tokens.shape[0] else body
        return form(tokens, expert_ids, *rest)

    return jax.shard_map(step, mesh=mesh, in_specs=in_specs, out_specs=out_specs, check_vma=False)
```

```python
import functools

import jax
import jax.numpy as jnp
from jax import lax
from jax.experimental import pallas as pl
from jax.experimental.pallas import tpu as pltpu
from jax.sharding import PartitionSpec as P

LANES = 128
TILE = 256
PARTS = 1
WIDE = (256, 256)
WIDE_STEPS = (1, 2, 3)
THIN = (512, 512)
EARLY_STEPS = (1, 2)


def from_partner(shard, axis, apart):
    return lax.ppermute(shard, axis, [(i, i ^ 1 << apart) for i in range(lax.axis_size(axis))])


def contract(left_op, right_op, left_dim, right_dim):
    return lax.dot_general(
        left_op,
        right_op,
        (((left_dim,), (right_dim,)), ((), ())),
        preferred_element_type=jnp.float32,
    )


def deliver(buffer, dp_size, ex_size, experts, capacity, backward):
    feat_width = buffer.shape[1]
    doubled = jnp.broadcast_to(
        buffer.reshape(experts, 1, capacity, feat_width), (experts, 2, capacity, feat_width)
    )
    doubled = doubled.reshape(dp_size, ex_size, capacity, feat_width)
    if backward:
        arrived = lax.all_to_all(
            lax.all_to_all(doubled, "dp", split_axis=0, concat_axis=0, tiled=True),
            "expert",
            split_axis=1,
            concat_axis=1,
            tiled=True,
        )
    else:
        arrived = lax.all_to_all(
            lax.all_to_all(doubled, "dp", split_axis=0, concat_axis=0, tiled=True),
            "expert",
            split_axis=1,
            concat_axis=1,
            tiled=True,
        )
    return arrived.reshape(-1, feat_width)


def bring_back(partials_in, dp_size, ex_size, experts, capacity, half_index, backward):
    feat_width = partials_in.shape[1]
    if backward:
        partner = from_partner(partials_in, "expert", 0)
    else:
        partner = from_partner(partials_in, "expert", 0)
    summed = (partials_in.astype(jnp.float32) + partner.astype(jnp.float32)).astype(jnp.bfloat16)
    summed = summed.reshape(dp_size, ex_size, capacity, feat_width)
    own_half = lax.dynamic_slice_in_dim(summed, half_index * (capacity // 2), capacity // 2, 2)
    if backward:
        returned = lax.all_to_all(
            lax.all_to_all(own_half, "dp", split_axis=0, concat_axis=0, tiled=True),
            "expert",
            split_axis=1,
            concat_axis=1,
            tiled=True,
        )
    else:
        returned = lax.all_to_all(
            lax.all_to_all(own_half, "dp", split_axis=0, concat_axis=0, tiled=True),
            "expert",
            split_axis=1,
            concat_axis=1,
            tiled=True,
        )
    merged = returned.reshape(experts, capacity, feat_width)
    return merged.reshape(experts * capacity, feat_width)


def body(tokens, expert_ids, route_weight, out_grad, gate_weight, up_weight, down_weight):
    dp_size = lax.axis_size("dp")
    ex_size = lax.axis_size("expert")
    tok_count, feat_width = tokens.shape
    top_count = expert_ids.shape[1]
    experts = dp_size * ex_size // 2
    assigned = tok_count * top_count
    capacity = 2 * (assigned // experts)
    half_index = lax.axis_index("expert") % 2
    flat_ids = expert_ids.reshape(-1)
    order = jnp.arange(assigned, dtype=jnp.int32)
    earlier = (flat_ids[:, None] == flat_ids[None, :]) & (order[None, :] < order[:, None])
    slot_ids = jnp.sum(earlier.astype(jnp.int32), axis=1)
    place_row = flat_ids * capacity + slot_ids
    source = (
        jnp.full((experts * capacity,), -1, jnp.int32)
        .at[place_row]
        .set(jnp.arange(assigned, dtype=jnp.int32))
    )
    filled = source >= 0
    assign = jnp.maximum(source, 0)
    rows_tok = assign // top_count
    send_rows = jnp.where(filled[:, None], tokens[rows_tok], jnp.zeros((), jnp.bfloat16))
    in_rows = deliver(send_rows, dp_size, ex_size, experts, capacity, False)
    w_gate = gate_weight[0]
    w_up = up_weight[0]
    w_down = down_weight[0]
    gate_act = jnp.dot(in_rows, w_gate, preferred_element_type=jnp.float32)
    up_act = jnp.dot(in_rows, w_up, preferred_element_type=jnp.float32)
    sig_gate = jax.nn.sigmoid(gate_act)
    hidden = (gate_act * sig_gate * up_act).astype(jnp.bfloat16)
    partial_value = jnp.dot(hidden, w_down, preferred_element_type=jnp.float32).astype(jnp.bfloat16)
    expert_table = bring_back(partial_value, dp_size, ex_size, experts, capacity, half_index, False)
    expert_rows = expert_table[place_row].reshape(tok_count, top_count, feat_width)
    layer_out = jnp.sum(route_weight[:, :, None] * expert_rows.astype(jnp.float32), axis=1).astype(
        jnp.bfloat16
    )
    route_grad = jnp.einsum("tkd,td->tk", expert_rows, out_grad, preferred_element_type=jnp.float32)
    scaled = (route_weight[:, :, None] * out_grad[:, None, :].astype(jnp.float32)).astype(
        jnp.bfloat16
    )
    scaled = scaled.reshape(assigned, feat_width)
    send_grad = jnp.where(filled[:, None], scaled[assign], jnp.zeros((), jnp.bfloat16))
    grad_rows = deliver(send_grad, dp_size, ex_size, experts, capacity, True)
    hidden_grad = contract(grad_rows, w_down, 1, 1)
    gate_pre = (hidden_grad * up_act * sig_gate * (1.0 + gate_act * (1.0 - sig_gate))).astype(
        jnp.bfloat16
    )
    up_pre = (hidden_grad * gate_act * sig_gate).astype(jnp.bfloat16)
    partial_grad = (contract(gate_pre, w_gate, 1, 1) + contract(up_pre, w_up, 1, 1)).astype(
        jnp.bfloat16
    )
    gate_grad = contract(in_rows, gate_pre, 0, 0).astype(jnp.bfloat16)
    up_grad = contract(in_rows, up_pre, 0, 0).astype(jnp.bfloat16)
    down_grad = contract(hidden, grad_rows, 0, 0).astype(jnp.bfloat16)
    grad_table = bring_back(partial_grad, dp_size, ex_size, experts, capacity, half_index, True)
    expert_grad = grad_table[place_row].reshape(tok_count, top_count, feat_width)
    token_grad = jnp.sum(expert_grad.astype(jnp.float32), axis=1).astype(jnp.bfloat16)
    return (layer_out, token_grad, route_grad, gate_grad[None], up_grad[None], down_grad[None])


def expert_kernel(
    planes, tok_count, width, half, experts, tile, wide, thin,
    tok_hbm, ids_hbm, rw_hbm, og_hbm, wg_hbm, wu_hbm, wd_hbm,
    lo_ref, tg_ref, rg_ref, gg_ref, ug_ref, dg_ref,
    ids_ref, rw_ref, rows, parts, swapped, summed, early, first_a, first_b, turn_a, turn_b, second_a, second_b,
    zsend, zrecv, zown, act_ref, hidden_all, pre_all, wgu_ref, wd_ref,
    load_sem, z_ss, z_rs, x_ss, x_rs, y_ss, y_rs, xh_ss, xh_rs, yh_ss, yh_rs, wide_ss, wide_rs,
    core_ss, core_rs, swap_ss, swap_rs, early_ss, early_rs, fa_ss, fa_rs, fb_ss, fb_rs,
    ta_ss, ta_rs, tb_ss, tb_rs, zo_ss, zo_rs,
):
    f32, bf16 = jnp.float32, jnp.bfloat16
    dp, ex = lax.axis_index("dp"), lax.axis_index("expert")
    z, y, x, c = dp // 2, dp % 2, ex // 2, ex % 2
    piece = dp * lax.axis_size("expert") + ex
    mine = piece // 2
    full = 2 * width + LANES
    x_dev, y_dev, core_dev = (dp, (1 - x) * 2 + c), (z * 2 + 1 - y, ex), (dp, x * 2 + 1 - c)
    left, right = pl.ds(0, width), pl.ds(width, width + LANES)
    gather_mid = pl.ds(wide[0], wide[1] - wide[0])
    gather_left, gather_right = pl.ds(0, wide[0]), pl.ds(wide[1], full - wide[1])
    reduce_mid = pl.ds(thin[0], thin[1] - thin[0])
    reduce_left, reduce_right = pl.ds(0, thin[0]), pl.ds(thin[1], full - thin[1])
    packed_right = pl.ds(thin[0], full - thin[1])

    def remote(src, dst, send, recv, device):
        return pltpu.make_async_remote_copy(
            src_ref=src, dst_ref=dst, send_sem=send, recv_sem=recv,
            device_id=device, device_id_type=pl.DeviceIdType.MESH,
        )

    def plane(step):
        return z ^ step

    def z_peer(q):
        return (q * 2 + y, ex)

    own_left = rows.at[z, c, 0, :, left]
    own_right = rows.at[z, c, 0, :, pl.ds(width, width)]
    loads = [
        pltpu.make_async_copy(src, dst, load_sem.at[i])
        for i, (src, dst) in enumerate(
            (
                (tok_hbm, own_left), (og_hbm, own_right), (ids_hbm, ids_ref), (rw_hbm, rw_ref),
                (wg_hbm.at[0], wgu_ref.at[:, pl.ds(0, half)]), (wu_hbm.at[0], wgu_ref.at[:, pl.ds(half, half)]),
                (wd_hbm.at[0], wd_ref),
            )
        )
    ]
    for load in loads:
        load.start()

    barrier = pltpu.get_barrier_semaphore()
    peers = [x_dev, y_dev, core_dev]
    peers += [z_peer((z + d) % planes) for d in range(1, planes)]
    for peer in peers:
        pl.semaphore_signal(barrier, inc=1, device_id=peer, device_id_type=pl.DeviceIdType.MESH)

    loads[0].wait()
    pl.semaphore_wait(barrier, len(peers))

    def z_copy(q, way, k):
        part = rows.at[q, c, 0, :, (left, right)[k]]
        return remote(part, part, z_ss.at[q, way, k], z_rs.at[q, k], z_peer(z + 1 - 2 * way))

    def relay(q, k, run):
        @pl.when((q <= z) & (z < planes - 1))
        def _():
            run(z_copy(q, 0, k))

        @pl.when((q >= z) & (z > 0))
        def _():
            run(z_copy(q, 1, k))

    def z_landed(q, k):
        part = rows.at[q, c, 0, :, (left, right)[k]]
        remote(part, part, z_ss.at[q, 0, k], z_rs.at[q, k], core_dev).wait_recv()

    def along(away, k):
        @pl.when(z >= away)
        def _():
            z_landed(z - away, k)
            relay(z - away, k, lambda copy: copy.start())

        @pl.when(z < planes - away)
        def _():
            z_landed(z + away, k)
            relay(z + away, k, lambda copy: copy.start())

    def gather_cols(s, k):
        return ((gather_left, gather_right) if s in WIDE_STEPS else (left, right))[k]

    def x_copy(s, k):
        cols = gather_cols(s, k)
        src, dst = rows.at[plane(s), c, 0, :, cols], rows.at[plane(s), c, 1, :, cols]
        return remote(src, dst, x_ss.at[s, k], x_rs.at[s, k], x_dev)

    def y_copy(s, k):
        cols = gather_cols(s, k)
        src, dst = rows.at[plane(s), c, 0, :, cols], rows.at[plane(s), c, 2, :, cols]
        return remote(src, dst, y_ss.at[s, k], y_rs.at[s, k], y_dev)

    def xh_copy(s):
        cols = gather_cols(s, 0)
        src, dst = rows.at[plane(s), c, 2, :, cols], rows.at[plane(s), c, 3, :, cols]
        return remote(src, dst, xh_ss.at[s], xh_rs.at[s], x_dev)

    def yh_copy(s):
        cols = gather_cols(s, 1)
        src, dst = rows.at[plane(s), c, 1, :, cols], rows.at[plane(s), c, 3, :, cols]
        return remote(src, dst, yh_ss.at[s], yh_rs.at[s], y_dev)

    def wide_slots(q, k):
        return rows.at[q, c, (pl.ds(1, 2), pl.ds(3, 1))[k], :, gather_mid]

    def wide_copy(s, k):
        slots = wide_slots(z, k)
        return remote(slots, slots, wide_ss.at[s - 1, k], wide_rs.at[z, k], z_peer(plane(s)))

    def wide_landed(q, k):
        slots = wide_slots(q, k)
        remote(slots, slots, wide_ss.at[0, k], wide_rs.at[q, k], core_dev).wait_recv()

    def core_copy(s, which, core):
        slots, cols = (
            (pl.ds(0, 1), pl.ds(0, full)), (pl.ds(1, 2), gather_left), (pl.ds(1, 2), gather_right),
            (pl.ds(3, 1), gather_left), (pl.ds(3, 1), gather_right), (pl.ds(1, 3), gather_mid),
        )[which]
        ref = rows.at[plane(s), core, slots, :, cols]
        return remote(ref, ref, core_ss.at[s, which], core_rs.at[s, which], core_dev)

    def whole(s):
        return s not in EARLY_STEPS

    def swap_copy(s, k):
        cols = (left, right)[k]
        src, dst = parts.at[s, 1 - c, :, :, cols], swapped.at[s, :, :, cols]
        return remote(src, dst, swap_ss.at[s, k], swap_rs.at[s, k], core_dev)

    def early_copy(s):
        src = summed.at[s, :, :, reduce_mid]
        return remote(src, early.at[z], early_ss.at[s], early_rs.at[z], z_peer(plane(s)))

    def early_landed(q):
        remote(early.at[q], early.at[q], early_ss.at[0], early_rs.at[q], core_dev).wait_recv()

    def fa_copy(s, own):
        last = whole(s)
        cols = left if last else reduce_left
        src, dst = summed.at[s, 1 if own else 3, :, cols], first_a.at[s, own, :, cols]
        return remote(src, dst, fa_ss.at[s, own], fa_rs.at[s, own], x_dev)

    def fb_copy(s, own):
        last = whole(s)
        cols = right if last else reduce_right
        at = pl.ds(0, width + LANES) if last else pl.ds(thin[1] - width, full - thin[1])
        src, dst = summed.at[s, 2 if own else 3, :, cols], first_b.at[s, own, :, at]
        return remote(src, dst, fb_ss.at[s, own], fb_rs.at[s, own], y_dev)

    def ta_copy(s):
        last = whole(s)
        at = pl.ds(0, width if last else thin[0])
        src, dst = turn_a.at[s, :, at], second_a.at[s, :, at]
        return remote(src, dst, ta_ss.at[s], ta_rs.at[s], y_dev)

    def tb_copy(s):
        last = whole(s)
        at = pl.ds(0, width + LANES) if last else pl.ds(thin[1] - width, full - thin[1])
        src, dst = turn_b.at[s, :, at], second_b.at[s, :, at]
        return remote(src, dst, tb_ss.at[s], tb_rs.at[s], x_dev)

    def zo_cols(s, k):
        if whole(s):
            return (left, right)[k]
        return (pl.ds(0, thin[0]), packed_right)[k]

    def zo_copy(s, k):
        cols = zo_cols(s, k)
        src, dst = zsend.at[s - 1, :, cols], zrecv.at[s - 1, :, cols]
        return remote(src, dst, zo_ss.at[s - 1, k], zo_rs.at[s - 1, k], z_peer(plane(s)))

    def pass_on(s, k):
        x_copy(s, k).start()
        y_copy(s, k).start()
        if k == 1:
            core_copy(s, 0, c).start()

    def across_x(s):
        y_copy(s, 0).wait_recv()
        xh_copy(s).start()

    def across_y(s):
        x_copy(s, 1).wait_recv()
        yh_copy(s).start()

    def to_core(s):
        x_copy(s, 0).wait_recv()
        core_copy(s, 1, c).start()
        y_copy(s, 1).wait_recv()
        core_copy(s, 2, c).start()

    def gathered(s):
        xh_copy(s).wait_recv()
        core_copy(s, 3, c).start()
        yh_copy(s).wait_recv()
        core_copy(s, 4, c).start()
        if s in WIDE_STEPS:
            wide_landed(plane(s), 0)
            wide_landed(plane(s), 1)
        core_copy(s, 5, c).start()

    def spread(k):
        for s in WIDE_STEPS:
            wide_copy(s, k).start()

    group = 8 * tok_count
    glane = lax.broadcasted_iota(jnp.int32, (group, LANES), 1)

    def group_at(s):
        return pl.ds(pl.multiple_of(plane(s) * group, group), group)

    def forward(s):
        q = plane(s)
        for which in range(6):
            core_copy(s, which, 1 - c).wait_recv()
        x_in = rows[q, :, :, :, 0:width].reshape(group, width)
        act_ref[...] = contract(x_in, wgu_ref[...], 1, 0)

    def middle(s):
        q = plane(s)
        g_in = rows[q, :, :, :, width : 2 * width].reshape(group, width)
        back = contract(g_in, wd_ref[...], 1, 1)
        gate, up = act_ref[:, 0:half], act_ref[:, half : 2 * half]
        tab = rows[q, :, :, :, 2 * width : full].reshape(group, LANES).astype(f32)
        own = (glane == mine) | (glane == mine + experts) | (glane == mine + 2 * experts)
        weight = jnp.sum(jnp.where(own, tab, 0.0), axis=1, keepdims=True)
        sig = 1.0 / (1.0 + jnp.exp(-gate))
        act = gate * sig
        hidden = act * up
        route = jnp.sum(hidden * back, axis=1, keepdims=True)
        coarse = route.astype(bf16).astype(f32)
        fine = route - coarse
        marks = jnp.where(glane == piece, coarse, jnp.where(glane == piece + LANES // 2, fine, 0.0))
        parts[s, :, :, :, 2 * width : full] = marks.astype(bf16).reshape(2, 4, tok_count, LANES)
        back = weight * back
        hidden_all[group_at(s), :] = (weight * hidden).astype(bf16)
        pre_all[group_at(s), 0:half] = (back * up * sig * (1.0 + gate * (1.0 - sig))).astype(bf16)
        pre_all[group_at(s), half : 2 * half] = (back * act).astype(bf16)

    def outward(s):
        hid = hidden_all[group_at(s), :]
        for n in range(0, width, 2 * tile):
            cols = slice(n, n + 2 * tile)
            out = contract(hid, wd_ref[:, cols], 1, 0)
            parts[s, :, :, :, cols] = out.astype(bf16).reshape(2, 4, tok_count, 2 * tile)
        swap_copy(s, 0).start()

    def inward(s, part):
        pre = pre_all[group_at(s), :]
        for n in range(part * width // 2, (part + 1) * width // 2, 2 * tile):
            cols = slice(n, n + 2 * tile)
            grad = contract(pre, wgu_ref[cols, :], 1, 1)
            after = slice(width + n, width + n + 2 * tile)
            parts[s, :, :, :, after] = grad.astype(bf16).reshape(2, 4, tok_count, 2 * tile)
        if part == 1:
            swap_copy(s, 1).start()

    def add_cores(s, cols):
        def add(t, carry):
            total = parts[s, c, t, :, cols].astype(f32) + swapped[s, t, :, cols].astype(f32)
            summed[s, t, :, cols] = total.astype(bf16)
            return carry

        lax.fori_loop(0, 4, add, 0)

    def reduce_left_half(s):
        swap_copy(s, 0).wait_recv()
        add_cores(s, left)
        for own in range(2):
            fa_copy(s, own).start()

    def reduce_right_half(s):
        swap_copy(s, 1).wait_recv()
        add_cores(s, right)
        for own in range(2):
            fb_copy(s, own).start()
        if s in EARLY_STEPS:
            early_copy(s).start()

    def add_own():
        swap_copy(0, 0).wait_recv()
        add_cores(0, reduce_left)
        swap_copy(0, 1).wait_recv()
        add_cores(0, reduce_right)

    def reduce_own():
        for s in EARLY_STEPS:
            early_landed(plane(s))

        def add(t, carry):
            total = parts[0, c, t, :, reduce_mid].astype(f32) + swapped[0, t, :, reduce_mid].astype(f32)
            for s in EARLY_STEPS:
                total = total + early[plane(s), t].astype(f32)
            summed[0, t, :, reduce_mid] = total.astype(bf16)
            return carry

        lax.fori_loop(0, 4, add, 0)
        for own in range(2):
            fa_copy(0, own).start()
            fb_copy(0, own).start()

    def turn_left(s):
        last = whole(s)
        fa_copy(s, 0).wait_recv()
        cols = slice(0, width if last else thin[0])
        total = summed[s, 2, :, cols].astype(f32) + first_a[s, 0, :, cols].astype(f32)
        turn_a[s, :, cols] = total.astype(bf16)
        ta_copy(s).start()

    def turn_right(s):
        last = whole(s)
        fb_copy(s, 0).wait_recv()
        begin = width if last else thin[1]
        at = slice(begin - width, full - width)
        total = summed[s, 1, :, begin:full].astype(f32) + first_b[s, 0, :, at].astype(f32)
        turn_b[s, :, at] = total.astype(bf16)
        tb_copy(s).start()

    def collect_left(s):
        fa_copy(s, 1).wait_recv()
        ta_copy(s).wait_recv()
        cols = slice(0, width if whole(s) else thin[0])
        total = summed[s, 0, :, cols].astype(f32) + first_a[s, 1, :, cols].astype(f32)
        total = total + second_a[s, :, cols].astype(f32)
        if s == 0:
            zown[:, cols] = total
        else:
            zsend[s - 1, :, cols] = total.astype(bf16)
            zo_copy(s, 0).start()

    def collect_right(s):
        fb_copy(s, 1).wait_recv()
        tb_copy(s).wait_recv()
        begin = width if whole(s) else thin[1]
        at = slice(begin - width, full - width)
        total = summed[s, 0, :, begin:full].astype(f32) + first_b[s, 1, :, at].astype(f32)
        total = total + second_b[s, :, at].astype(f32)
        if s == 0:
            zown[:, width:full] = total
        else:
            zsend[s - 1, :, zo_cols(s, 1)] = total.astype(bf16)
            zo_copy(s, 1).start()

    every = planes * group
    tiles = width // tile

    def weight_grads(t):
        cols = pl.ds(t * tile, tile)
        x_in = rows[:, :, :, :, cols].reshape(every, tile)
        after = pl.ds(width + t * tile, tile)
        g_in = rows[:, :, :, :, after].reshape(every, tile)
        both = contract(x_in, pre_all[...], 0, 0).astype(bf16)
        gg_ref[0, cols, :] = both[:, 0:half]
        ug_ref[0, cols, :] = both[:, half : 2 * half]
        dg_ref[0, :, cols] = contract(hidden_all[...], g_in, 0, 0).astype(bf16)

    def weights_ready():
        for load in loads[4:]:
            load.wait()

    relay(z, 0, lambda copy: copy.start())
    y_copy(0, 0).start()
    x_copy(0, 0).start()
    loads[2].wait()
    loads[3].wait()
    lane = lax.broadcasted_iota(jnp.int32, (tok_count, LANES), 1)
    ids, weights = ids_ref[...].T, rw_ref[...].T
    table = [jnp.zeros((tok_count, LANES), f32) for _ in range(3)]
    for k in range(ids.shape[1]):
        for part in range(3):
            hit = lane == ids[:, k : k + 1] + part * experts
            table[part] = jnp.where(hit, weights[:, k : k + 1], table[part])
    head = table[0].astype(bf16).astype(f32)
    mid = table[1] - table[1].astype(bf16).astype(f32)
    mid = mid.astype(bf16).astype(f32)
    rest = table[2] - table[2].astype(bf16).astype(f32)
    rest = rest - rest.astype(bf16).astype(f32)
    rows[z, c, 0, :, pl.ds(2 * width, LANES)] = (head + mid + rest).astype(bf16)
    loads[1].wait()
    relay(z, 1, lambda copy: copy.start())
    x_copy(0, 1).start()
    y_copy(0, 1).start()
    core_copy(0, 0, c).start()
    along(1, 0)
    pass_on(1, 0)
    across_y(0)
    across_x(0)
    along(1, 1)
    pass_on(1, 1)
    along(2, 0)
    to_core(0)
    pass_on(2, 0)
    gathered(0)
    along(2, 1)
    pass_on(2, 1)
    weights_ready()
    spread(0)
    across_y(1)
    across_x(1)
    forward(0)
    middle(0)
    spread(1)
    across_x(2)
    along(3, 0)
    pass_on(3, 0)
    across_y(2)
    to_core(2)
    to_core(1)
    gathered(1)
    along(3, 1)
    pass_on(3, 1)
    forward(1)
    middle(1)
    outward(1)
    gathered(2)
    across_x(3)
    inward(1, 0)
    inward(1, 1)
    across_y(3)
    reduce_left_half(1)
    forward(2)
    middle(2)
    outward(2)
    to_core(3)
    reduce_right_half(1)
    inward(2, 0)
    inward(2, 1)
    reduce_left_half(2)
    gathered(3)
    inward(0, 0)
    inward(0, 1)
    reduce_right_half(2)
    forward(3)
    middle(3)
    turn_right(1)
    inward(3, 0)
    inward(3, 1)
    turn_left(2)
    outward(3)
    turn_right(2)
    reduce_right_half(3)
    reduce_left_half(3)
    outward(0)
    collect_left(2)
    add_own()
    turn_right(3)
    collect_right(2)
    turn_left(1)
    turn_left(3)
    weight_grads(0)
    weight_grads(1)
    collect_right(1)
    reduce_own()
    collect_right(3)
    collect_left(1)
    collect_left(3)
    weight_grads(4)
    weight_grads(5)
    turn_right(0)
    turn_left(0)
    weight_grads(6)
    weight_grads(7)
    weight_grads(2)
    weight_grads(3)
    collect_left(0)
    collect_right(0)
    for s in range(planes):
        for k in range(2):
            x_copy(s, k).wait_send()
            y_copy(s, k).wait_send()
            swap_copy(s, k).wait_send()
            fa_copy(s, k).wait_send()
            fb_copy(s, k).wait_send()
            relay(plane(s), k, lambda copy: copy.wait_send())
            if s in WIDE_STEPS:
                wide_copy(s, k).wait_send()
        if s in EARLY_STEPS:
            early_copy(s).wait_send()
        xh_copy(s).wait_send()
        yh_copy(s).wait_send()
        for which in range(6):
            core_copy(s, which, c).wait_send()
        ta_copy(s).wait_send()
        tb_copy(s).wait_send()

    def total(k):
        out = zown[:, 0:width] if k == 0 else zown[:, width:full]
        ends = (width - thin[0], thin[1] - width)
        for s in range(1, planes):
            zo_copy(s, k).wait_recv()
            more = zrecv[s - 1, :, zo_cols(s, k)].astype(f32)
            if not whole(s):
                pad = jnp.zeros((tok_count, ends[k]), f32)
                more = jnp.concatenate([more, pad] if k == 0 else [pad, more], axis=1)
            out = out + more
        return out

    lo_ref[...] = total(0).astype(bf16)
    total_b = total(1)
    tg_ref[...] = total_b[:, 0:width].astype(bf16)
    marks = total_b[:, width:]
    routes = jnp.zeros((tok_count, LANES), f32)
    for k in range(ids.shape[1]):
        base = 2 * ids[:, k : k + 1]
        hit = (lane == base) | (lane == base + 1)
        hit = hit | (lane == base + LANES // 2) | (lane == base + LANES // 2 + 1)
        value = jnp.sum(jnp.where(hit, marks, 0.0), axis=1, keepdims=True)
        routes = jnp.where(lane == k, value, routes)
    rg_ref[...] = routes.T[0 : ids.shape[1], :]
    for s in range(1, planes):
        for k in range(2):
            zo_copy(s, k).wait_send()


def finish_kernel(
    lo_in, tg_in, rg_in, gg_in, ug_in, dg_in, lo_ref, tg_ref, rg_ref, gg_ref, ug_ref, dg_ref, out_sem, small_sem
):
    copies = []
    for i, (src, dst) in enumerate(((gg_in, gg_ref), (ug_in, ug_ref), (dg_in, dg_ref))):
        count = src.shape[1] // PARTS
        for j in range(PARTS):
            at = pl.ds(j * count, count)
            copies.append(pltpu.make_async_copy(src.at[0, at, :], dst.at[0, at, :], out_sem.at[i, j]))
    for i, (src, dst) in enumerate(((lo_in, lo_ref), (tg_in, tg_ref), (rg_in, rg_ref))):
        copies.append(pltpu.make_async_copy(src, dst, small_sem.at[i]))
    for copy in copies:
        copy.start()
    for copy in copies:
        copy.wait()


def kernel_body(tokens, expert_ids, route_weight, out_grad, gate_weight, up_weight, down_weight):
    dp_size, ex_size = lax.axis_size("dp"), lax.axis_size("expert")
    planes, experts = dp_size // 2, dp_size * ex_size // 2
    tok_count, width = tokens.shape
    half = gate_weight.shape[2]
    tile = TILE
    full = 2 * width + LANES
    wide = (width - WIDE[0], width + WIDE[1])
    thin = (width - THIN[0], width + THIN[1])
    bf16, f32 = jnp.bfloat16, jnp.float32
    every = planes * 8 * tok_count
    dma = pltpu.SemaphoreType.DMA
    vmem = pl.BlockSpec(memory_space=pltpu.VMEM)
    hbm = pl.BlockSpec(memory_space=pltpu.HBM)
    shape = jax.ShapeDtypeStruct
    several = lambda *counts: [dma(counts), dma(counts)]
    sems = [dma((7,)), dma((planes, 2, 2)), dma((planes, 2))]
    sems += several(planes, 2) * 2 + several(planes) * 2 + [dma((planes - 1, 2)), dma((planes, 2))]
    sems += several(planes, 6) + several(planes, 2) + several(planes) + several(planes, 2) * 2
    sems += several(planes) * 2 + several(planes - 1, 2)
    outs = pl.pallas_call(
        functools.partial(expert_kernel, planes, tok_count, width, half, experts, tile, wide, thin),
        out_shape=(
            pltpu.VMEM(tokens.shape, bf16),
            pltpu.VMEM(tokens.shape, bf16),
            pltpu.VMEM(route_weight.shape[::-1], f32),
            pltpu.VMEM(gate_weight.shape, bf16),
            pltpu.VMEM(up_weight.shape, bf16),
            pltpu.VMEM(down_weight.shape, bf16),
        ),
        in_specs=[hbm] * 7,
        out_specs=[vmem] * 6,
        scratch_shapes=[
            pltpu.VMEM(expert_ids.shape[::-1], jnp.int32),
            pltpu.VMEM(route_weight.shape[::-1], f32),
            pltpu.VMEM((planes, 2, 4, tok_count, full), bf16),
            pltpu.VMEM((planes, 2, 4, tok_count, full), bf16),
            pltpu.VMEM((planes, 4, tok_count, full), bf16),
            pltpu.VMEM((planes, 4, tok_count, full), bf16),
            pltpu.VMEM((planes, 4, tok_count, thin[1] - thin[0]), bf16),
            pltpu.VMEM((planes, 2, tok_count, width), bf16),
            pltpu.VMEM((planes, 2, tok_count, width + LANES), bf16),
            pltpu.VMEM((planes, tok_count, width), bf16),
            pltpu.VMEM((planes, tok_count, width + LANES), bf16),
            pltpu.VMEM((planes, tok_count, width), bf16),
            pltpu.VMEM((planes, tok_count, width + LANES), bf16),
            pltpu.VMEM((planes - 1, tok_count, full), bf16),
            pltpu.VMEM((planes - 1, tok_count, full), bf16),
            pltpu.VMEM((tok_count, full), f32),
            pltpu.VMEM((8 * tok_count, 2 * half), f32),
            pltpu.VMEM((every, half), bf16),
            pltpu.VMEM((every, 2 * half), bf16),
            pltpu.VMEM((width, 2 * half), bf16),
            pltpu.VMEM(down_weight.shape[1:], bf16),
        ] + sems,
        compiler_params=pltpu.CompilerParams(
            collective_id=0, has_side_effects=True, vmem_limit_bytes=60620 * 1024
        ),
    )(tokens, expert_ids.T, route_weight.T, out_grad, gate_weight, up_weight, down_weight)
    lo, tg, rg, gg, ug, dg = pl.pallas_call(
        finish_kernel,
        out_shape=tuple(shape(o.shape, o.dtype) for o in outs),
        in_specs=[vmem] * 6,
        out_specs=[hbm] * 6,
        scratch_shapes=[dma((3, PARTS)), dma((3,))],
        compiler_params=pltpu.CompilerParams(vmem_limit_bytes=4 * 1024 * 1024),
    )(*outs)
    return lo, tg, rg.T, gg, ug, dg


def solution(mesh):
    in_specs = (
        P(("dp", "expert"), None),
        P(("dp", "expert"), None),
        P(("dp", "expert"), None),
        P(("dp", "expert"), None),
        P(("dp", "expert"), None, None),
        P(("dp", "expert"), None, None),
        P(("dp", "expert"), None, None),
    )
    out_specs = (
        P(("dp", "expert"), None),
        P(("dp", "expert"), None),
        P(("dp", "expert"), None),
        P(("dp", "expert"), None, None),
        P(("dp", "expert"), None, None),
        P(("dp", "expert"), None, None),
    )
    dp_size, ex_size = mesh.shape["dp"], mesh.shape["expert"]
    pieces = dp_size * ex_size

    def step(tokens, expert_ids, *rest):
        capacity = 2 * (tokens.shape[0] * expert_ids.shape[1] // (pieces // 2))
        fits = ex_size == 4 and dp_size == 8 and 3 * pieces // 2 <= LANES
        fits = fits and pieces <= LANES // 2 and tokens.shape[1] % (2 * TILE) == 0
        fits = fits and tokens.shape[1] > max(WIDE + THIN)
        form = kernel_body if fits and capacity >= tokens.shape[0] else body
        return form(tokens, expert_ids, *rest)

    return jax.shard_map(step, mesh=mesh, in_specs=in_specs, out_specs=out_specs, check_vma=False)
```

```python
import functools

import jax
import jax.numpy as jnp
from jax import lax
from jax.experimental import pallas as pl
from jax.experimental.pallas import tpu as pltpu
from jax.sharding import PartitionSpec as P

LANES = 128
TILE = 256
PARTS = 1
WIDE = (256, 384)
WIDE_STEPS = (1, 2, 3)
THIN = (512, 512)
EARLY_STEPS = (1, 2)


def from_partner(shard, axis, apart):
    return lax.ppermute(shard, axis, [(i, i ^ 1 << apart) for i in range(lax.axis_size(axis))])


def contract(left_op, right_op, left_dim, right_dim):
    return lax.dot_general(
        left_op,
        right_op,
        (((left_dim,), (right_dim,)), ((), ())),
        preferred_element_type=jnp.float32,
    )


def deliver(buffer, dp_size, ex_size, experts, capacity, backward):
    feat_width = buffer.shape[1]
    doubled = jnp.broadcast_to(
        buffer.reshape(experts, 1, capacity, feat_width), (experts, 2, capacity, feat_width)
    )
    doubled = doubled.reshape(dp_size, ex_size, capacity, feat_width)
    if backward:
        arrived = lax.all_to_all(
            lax.all_to_all(doubled, "dp", split_axis=0, concat_axis=0, tiled=True),
            "expert",
            split_axis=1,
            concat_axis=1,
            tiled=True,
        )
    else:
        arrived = lax.all_to_all(
            lax.all_to_all(doubled, "dp", split_axis=0, concat_axis=0, tiled=True),
            "expert",
            split_axis=1,
            concat_axis=1,
            tiled=True,
        )
    return arrived.reshape(-1, feat_width)


def bring_back(partials_in, dp_size, ex_size, experts, capacity, half_index, backward):
    feat_width = partials_in.shape[1]
    if backward:
        partner = from_partner(partials_in, "expert", 0)
    else:
        partner = from_partner(partials_in, "expert", 0)
    summed = (partials_in.astype(jnp.float32) + partner.astype(jnp.float32)).astype(jnp.bfloat16)
    summed = summed.reshape(dp_size, ex_size, capacity, feat_width)
    own_half = lax.dynamic_slice_in_dim(summed, half_index * (capacity // 2), capacity // 2, 2)
    if backward:
        returned = lax.all_to_all(
            lax.all_to_all(own_half, "dp", split_axis=0, concat_axis=0, tiled=True),
            "expert",
            split_axis=1,
            concat_axis=1,
            tiled=True,
        )
    else:
        returned = lax.all_to_all(
            lax.all_to_all(own_half, "dp", split_axis=0, concat_axis=0, tiled=True),
            "expert",
            split_axis=1,
            concat_axis=1,
            tiled=True,
        )
    merged = returned.reshape(experts, capacity, feat_width)
    return merged.reshape(experts * capacity, feat_width)


def body(tokens, expert_ids, route_weight, out_grad, gate_weight, up_weight, down_weight):
    dp_size = lax.axis_size("dp")
    ex_size = lax.axis_size("expert")
    tok_count, feat_width = tokens.shape
    top_count = expert_ids.shape[1]
    experts = dp_size * ex_size // 2
    assigned = tok_count * top_count
    capacity = 2 * (assigned // experts)
    half_index = lax.axis_index("expert") % 2
    flat_ids = expert_ids.reshape(-1)
    order = jnp.arange(assigned, dtype=jnp.int32)
    earlier = (flat_ids[:, None] == flat_ids[None, :]) & (order[None, :] < order[:, None])
    slot_ids = jnp.sum(earlier.astype(jnp.int32), axis=1)
    place_row = flat_ids * capacity + slot_ids
    source = (
        jnp.full((experts * capacity,), -1, jnp.int32)
        .at[place_row]
        .set(jnp.arange(assigned, dtype=jnp.int32))
    )
    filled = source >= 0
    assign = jnp.maximum(source, 0)
    rows_tok = assign // top_count
    send_rows = jnp.where(filled[:, None], tokens[rows_tok], jnp.zeros((), jnp.bfloat16))
    in_rows = deliver(send_rows, dp_size, ex_size, experts, capacity, False)
    w_gate = gate_weight[0]
    w_up = up_weight[0]
    w_down = down_weight[0]
    gate_act = jnp.dot(in_rows, w_gate, preferred_element_type=jnp.float32)
    up_act = jnp.dot(in_rows, w_up, preferred_element_type=jnp.float32)
    sig_gate = jax.nn.sigmoid(gate_act)
    hidden = (gate_act * sig_gate * up_act).astype(jnp.bfloat16)
    partial_value = jnp.dot(hidden, w_down, preferred_element_type=jnp.float32).astype(jnp.bfloat16)
    expert_table = bring_back(partial_value, dp_size, ex_size, experts, capacity, half_index, False)
    expert_rows = expert_table[place_row].reshape(tok_count, top_count, feat_width)
    layer_out = jnp.sum(route_weight[:, :, None] * expert_rows.astype(jnp.float32), axis=1).astype(
        jnp.bfloat16
    )
    route_grad = jnp.einsum("tkd,td->tk", expert_rows, out_grad, preferred_element_type=jnp.float32)
    scaled = (route_weight[:, :, None] * out_grad[:, None, :].astype(jnp.float32)).astype(
        jnp.bfloat16
    )
    scaled = scaled.reshape(assigned, feat_width)
    send_grad = jnp.where(filled[:, None], scaled[assign], jnp.zeros((), jnp.bfloat16))
    grad_rows = deliver(send_grad, dp_size, ex_size, experts, capacity, True)
    hidden_grad = contract(grad_rows, w_down, 1, 1)
    gate_pre = (hidden_grad * up_act * sig_gate * (1.0 + gate_act * (1.0 - sig_gate))).astype(
        jnp.bfloat16
    )
    up_pre = (hidden_grad * gate_act * sig_gate).astype(jnp.bfloat16)
    partial_grad = (contract(gate_pre, w_gate, 1, 1) + contract(up_pre, w_up, 1, 1)).astype(
        jnp.bfloat16
    )
    gate_grad = contract(in_rows, gate_pre, 0, 0).astype(jnp.bfloat16)
    up_grad = contract(in_rows, up_pre, 0, 0).astype(jnp.bfloat16)
    down_grad = contract(hidden, grad_rows, 0, 0).astype(jnp.bfloat16)
    grad_table = bring_back(partial_grad, dp_size, ex_size, experts, capacity, half_index, True)
    expert_grad = grad_table[place_row].reshape(tok_count, top_count, feat_width)
    token_grad = jnp.sum(expert_grad.astype(jnp.float32), axis=1).astype(jnp.bfloat16)
    return (layer_out, token_grad, route_grad, gate_grad[None], up_grad[None], down_grad[None])


def expert_kernel(
    planes, tok_count, width, half, experts, tile, wide, thin,
    tok_hbm, ids_hbm, rw_hbm, og_hbm, wg_hbm, wu_hbm, wd_hbm,
    lo_ref, tg_ref, rg_ref, gg_ref, ug_ref, dg_ref,
    ids_ref, rw_ref, rows, parts, swapped, summed, early, first_a, first_b, turn_a, turn_b, second_a, second_b,
    zsend, zrecv, zown, act_ref, hidden_all, pre_all, wgu_ref, wd_ref,
    load_sem, z_ss, z_rs, x_ss, x_rs, y_ss, y_rs, xh_ss, xh_rs, yh_ss, yh_rs, wide_ss, wide_rs,
    core_ss, core_rs, swap_ss, swap_rs, early_ss, early_rs, fa_ss, fa_rs, fb_ss, fb_rs,
    ta_ss, ta_rs, tb_ss, tb_rs, zo_ss, zo_rs,
):
    f32, bf16 = jnp.float32, jnp.bfloat16
    dp, ex = lax.axis_index("dp"), lax.axis_index("expert")
    z, y, x, c = dp // 2, dp % 2, ex // 2, ex % 2
    piece = dp * lax.axis_size("expert") + ex
    mine = piece // 2
    full = 2 * width + LANES
    x_dev, y_dev, core_dev = (dp, (1 - x) * 2 + c), (z * 2 + 1 - y, ex), (dp, x * 2 + 1 - c)
    left, right = pl.ds(0, width), pl.ds(width, width + LANES)
    gather_mid = pl.ds(wide[0], wide[1] - wide[0])
    gather_left, gather_right = pl.ds(0, wide[0]), pl.ds(wide[1], full - wide[1])
    reduce_mid = pl.ds(thin[0], thin[1] - thin[0])
    reduce_left, reduce_right = pl.ds(0, thin[0]), pl.ds(thin[1], full - thin[1])
    packed_right = pl.ds(thin[0], full - thin[1])

    def remote(src, dst, send, recv, device):
        return pltpu.make_async_remote_copy(
            src_ref=src, dst_ref=dst, send_sem=send, recv_sem=recv,
            device_id=device, device_id_type=pl.DeviceIdType.MESH,
        )

    def plane(step):
        return z ^ step

    def z_peer(q):
        return (q * 2 + y, ex)

    barrier = pltpu.get_barrier_semaphore()
    peers = [x_dev, y_dev, core_dev]
    peers += [z_peer((z + d) % planes) for d in range(1, planes)]
    for peer in peers:
        pl.semaphore_signal(barrier, inc=1, device_id=peer, device_id_type=pl.DeviceIdType.MESH)

    own_left = rows.at[z, c, 0, :, left]
    own_right = rows.at[z, c, 0, :, pl.ds(width, width)]
    loads = [
        pltpu.make_async_copy(src, dst, load_sem.at[i])
        for i, (src, dst) in enumerate(
            (
                (tok_hbm, own_left), (og_hbm, own_right), (ids_hbm, ids_ref), (rw_hbm, rw_ref),
                (wg_hbm.at[0], wgu_ref.at[:, pl.ds(0, half)]), (wu_hbm.at[0], wgu_ref.at[:, pl.ds(half, half)]),
                (wd_hbm.at[0], wd_ref),
            )
        )
    ]
    for load in loads:
        load.start()

    loads[0].wait()
    pl.semaphore_wait(barrier, len(peers))

    def z_copy(q, way, k):
        part = rows.at[q, c, 0, :, (left, right)[k]]
        return remote(part, part, z_ss.at[q, way, k], z_rs.at[q, k], z_peer(z + 1 - 2 * way))

    def relay(q, k, run):
        @pl.when((q <= z) & (z < planes - 1))
        def _():
            run(z_copy(q, 0, k))

        @pl.when((q >= z) & (z > 0))
        def _():
            run(z_copy(q, 1, k))

    def z_landed(q, k):
        part = rows.at[q, c, 0, :, (left, right)[k]]
        remote(part, part, z_ss.at[q, 0, k], z_rs.at[q, k], core_dev).wait_recv()

    def along(away, k):
        @pl.when(z >= away)
        def _():
            z_landed(z - away, k)
            relay(z - away, k, lambda copy: copy.start())

        @pl.when(z < planes - away)
        def _():
            z_landed(z + away, k)
            relay(z + away, k, lambda copy: copy.start())

    def gather_cols(s, k):
        return ((gather_left, gather_right) if s in WIDE_STEPS else (left, right))[k]

    def x_copy(s, k):
        cols = gather_cols(s, k)
        src, dst = rows.at[plane(s), c, 0, :, cols], rows.at[plane(s), c, 1, :, cols]
        return remote(src, dst, x_ss.at[s, k], x_rs.at[s, k], x_dev)

    def y_copy(s, k):
        cols = gather_cols(s, k)
        src, dst = rows.at[plane(s), c, 0, :, cols], rows.at[plane(s), c, 2, :, cols]
        return remote(src, dst, y_ss.at[s, k], y_rs.at[s, k], y_dev)

    def xh_copy(s):
        cols = gather_cols(s, 0)
        src, dst = rows.at[plane(s), c, 2, :, cols], rows.at[plane(s), c, 3, :, cols]
        return remote(src, dst, xh_ss.at[s], xh_rs.at[s], x_dev)

    def yh_copy(s):
        cols = gather_cols(s, 1)
        src, dst = rows.at[plane(s), c, 1, :, cols], rows.at[plane(s), c, 3, :, cols]
        return remote(src, dst, yh_ss.at[s], yh_rs.at[s], y_dev)

    def wide_slots(q, k):
        return rows.at[q, c, (pl.ds(1, 2), pl.ds(3, 1))[k], :, gather_mid]

    def wide_copy(s, k):
        slots = wide_slots(z, k)
        return remote(slots, slots, wide_ss.at[s - 1, k], wide_rs.at[z, k], z_peer(plane(s)))

    def wide_landed(q, k):
        slots = wide_slots(q, k)
        remote(slots, slots, wide_ss.at[0, k], wide_rs.at[q, k], core_dev).wait_recv()

    def core_copy(s, which, core):
        slots, cols = (
            (pl.ds(0, 1), pl.ds(0, full)), (pl.ds(1, 2), gather_left), (pl.ds(1, 2), gather_right),
            (pl.ds(3, 1), gather_left), (pl.ds(3, 1), gather_right), (pl.ds(1, 3), gather_mid),
        )[which]
        ref = rows.at[plane(s), core, slots, :, cols]
        return remote(ref, ref, core_ss.at[s, which], core_rs.at[s, which], core_dev)

    def whole(s):
        return s not in EARLY_STEPS

    def swap_copy(s, k):
        cols = (left, right)[k]
        src, dst = parts.at[s, 1 - c, :, :, cols], swapped.at[s, :, :, cols]
        return remote(src, dst, swap_ss.at[s, k], swap_rs.at[s, k], core_dev)

    def early_copy(s):
        src = summed.at[s, :, :, reduce_mid]
        return remote(src, early.at[z], early_ss.at[s], early_rs.at[z], z_peer(plane(s)))

    def early_landed(q):
        remote(early.at[q], early.at[q], early_ss.at[0], early_rs.at[q], core_dev).wait_recv()

    def fa_copy(s, own):
        last = whole(s)
        cols = left if last else reduce_left
        src, dst = summed.at[s, 1 if own else 3, :, cols], first_a.at[s, own, :, cols]
        return remote(src, dst, fa_ss.at[s, own], fa_rs.at[s, own], x_dev)

    def fb_copy(s, own):
        last = whole(s)
        cols = right if last else reduce_right
        at = pl.ds(0, width + LANES) if last else pl.ds(thin[1] - width, full - thin[1])
        src, dst = summed.at[s, 2 if own else 3, :, cols], first_b.at[s, own, :, at]
        return remote(src, dst, fb_ss.at[s, own], fb_rs.at[s, own], y_dev)

    def ta_copy(s):
        last = whole(s)
        at = pl.ds(0, width if last else thin[0])
        src, dst = turn_a.at[s, :, at], second_a.at[s, :, at]
        return remote(src, dst, ta_ss.at[s], ta_rs.at[s], y_dev)

    def tb_copy(s):
        last = whole(s)
        at = pl.ds(0, width + LANES) if last else pl.ds(thin[1] - width, full - thin[1])
        src, dst = turn_b.at[s, :, at], second_b.at[s, :, at]
        return remote(src, dst, tb_ss.at[s], tb_rs.at[s], x_dev)

    def zo_cols(s, k):
        if whole(s):
            return (left, right)[k]
        return (pl.ds(0, thin[0]), packed_right)[k]

    def zo_copy(s, k):
        cols = zo_cols(s, k)
        src, dst = zsend.at[s - 1, :, cols], zrecv.at[s - 1, :, cols]
        return remote(src, dst, zo_ss.at[s - 1, k], zo_rs.at[s - 1, k], z_peer(plane(s)))

    def pass_on(s, k):
        x_copy(s, k).start()
        y_copy(s, k).start()
        if k == 1:
            core_copy(s, 0, c).start()

    def across_x(s):
        y_copy(s, 0).wait_recv()
        xh_copy(s).start()

    def across_y(s):
        x_copy(s, 1).wait_recv()
        yh_copy(s).start()

    def to_core(s):
        x_copy(s, 0).wait_recv()
        core_copy(s, 1, c).start()
        y_copy(s, 1).wait_recv()
        core_copy(s, 2, c).start()

    def gathered(s):
        xh_copy(s).wait_recv()
        core_copy(s, 3, c).start()
        yh_copy(s).wait_recv()
        core_copy(s, 4, c).start()
        if s in WIDE_STEPS:
            wide_landed(plane(s), 0)
            wide_landed(plane(s), 1)
        core_copy(s, 5, c).start()

    def spread(k):
        for s in WIDE_STEPS:
            wide_copy(s, k).start()

    group = 8 * tok_count
    glane = lax.broadcasted_iota(jnp.int32, (group, LANES), 1)

    def group_at(s):
        return pl.ds(pl.multiple_of(plane(s) * group, group), group)

    def forward(s):
        q = plane(s)
        for which in range(6):
            core_copy(s, which, 1 - c).wait_recv()
        x_in = rows[q, :, :, :, 0:width].reshape(group, width)
        act_ref[...] = contract(x_in, wgu_ref[...], 1, 0)

    def middle(s):
        q = plane(s)
        g_in = rows[q, :, :, :, width : 2 * width].reshape(group, width)
        back = contract(g_in, wd_ref[...], 1, 1)
        gate, up = act_ref[:, 0:half], act_ref[:, half : 2 * half]
        tab = rows[q, :, :, :, 2 * width : full].reshape(group, LANES).astype(f32)
        own = (glane == mine) | (glane == mine + experts) | (glane == mine + 2 * experts)
        weight = jnp.sum(jnp.where(own, tab, 0.0), axis=1, keepdims=True)
        sig = 1.0 / (1.0 + jnp.exp(-gate))
        act = gate * sig
        hidden = act * up
        route = jnp.sum(hidden * back, axis=1, keepdims=True)
        coarse = route.astype(bf16).astype(f32)
        fine = route - coarse
        marks = jnp.where(glane == piece, coarse, jnp.where(glane == piece + LANES // 2, fine, 0.0))
        parts[s, :, :, :, 2 * width : full] = marks.astype(bf16).reshape(2, 4, tok_count, LANES)
        back = weight * back
        hidden_all[group_at(s), :] = (weight * hidden).astype(bf16)
        pre_all[group_at(s), 0:half] = (back * up * sig * (1.0 + gate * (1.0 - sig))).astype(bf16)
        pre_all[group_at(s), half : 2 * half] = (back * act).astype(bf16)

    def outward(s):
        hid = hidden_all[group_at(s), :]
        for n in range(0, width, 2 * tile):
            cols = slice(n, n + 2 * tile)
            out = contract(hid, wd_ref[:, cols], 1, 0)
            parts[s, :, :, :, cols] = out.astype(bf16).reshape(2, 4, tok_count, 2 * tile)
        swap_copy(s, 0).start()

    def inward(s, part):
        pre = pre_all[group_at(s), :]
        for n in range(part * width // 2, (part + 1) * width // 2, 2 * tile):
            cols = slice(n, n + 2 * tile)
            grad = contract(pre, wgu_ref[cols, :], 1, 1)
            after = slice(width + n, width + n + 2 * tile)
            parts[s, :, :, :, after] = grad.astype(bf16).reshape(2, 4, tok_count, 2 * tile)
        if part == 1:
            swap_copy(s, 1).start()

    def add_cores(s, cols):
        def add(t, carry):
            total = parts[s, c, t, :, cols].astype(f32) + swapped[s, t, :, cols].astype(f32)
            summed[s, t, :, cols] = total.astype(bf16)
            return carry

        lax.fori_loop(0, 4, add, 0)

    def reduce_left_half(s):
        swap_copy(s, 0).wait_recv()
        add_cores(s, left)
        for own in range(2):
            fa_copy(s, own).start()

    def reduce_right_half(s):
        swap_copy(s, 1).wait_recv()
        add_cores(s, right)
        for own in range(2):
            fb_copy(s, own).start()
        if s in EARLY_STEPS:
            early_copy(s).start()

    def add_own():
        swap_copy(0, 0).wait_recv()
        add_cores(0, reduce_left)
        swap_copy(0, 1).wait_recv()
        add_cores(0, reduce_right)

    def reduce_own():
        for s in EARLY_STEPS:
            early_landed(plane(s))

        def add(t, carry):
            total = parts[0, c, t, :, reduce_mid].astype(f32) + swapped[0, t, :, reduce_mid].astype(f32)
            for s in EARLY_STEPS:
                total = total + early[plane(s), t].astype(f32)
            summed[0, t, :, reduce_mid] = total.astype(bf16)
            return carry

        lax.fori_loop(0, 4, add, 0)
        for own in range(2):
            fa_copy(0, own).start()
            fb_copy(0, own).start()

    def turn_left(s):
        last = whole(s)
        fa_copy(s, 0).wait_recv()
        cols = slice(0, width if last else thin[0])
        total = summed[s, 2, :, cols].astype(f32) + first_a[s, 0, :, cols].astype(f32)
        turn_a[s, :, cols] = total.astype(bf16)
        ta_copy(s).start()

    def turn_right(s):
        last = whole(s)
        fb_copy(s, 0).wait_recv()
        begin = width if last else thin[1]
        at = slice(begin - width, full - width)
        total = summed[s, 1, :, begin:full].astype(f32) + first_b[s, 0, :, at].astype(f32)
        turn_b[s, :, at] = total.astype(bf16)
        tb_copy(s).start()

    def collect_left(s):
        fa_copy(s, 1).wait_recv()
        ta_copy(s).wait_recv()
        cols = slice(0, width if whole(s) else thin[0])
        total = summed[s, 0, :, cols].astype(f32) + first_a[s, 1, :, cols].astype(f32)
        total = total + second_a[s, :, cols].astype(f32)
        if s == 0:
            zown[:, cols] = total
        else:
            zsend[s - 1, :, cols] = total.astype(bf16)
            zo_copy(s, 0).start()

    def collect_right(s):
        fb_copy(s, 1).wait_recv()
        tb_copy(s).wait_recv()
        begin = width if whole(s) else thin[1]
        at = slice(begin - width, full - width)
        total = summed[s, 0, :, begin:full].astype(f32) + first_b[s, 1, :, at].astype(f32)
        total = total + second_b[s, :, at].astype(f32)
        if s == 0:
            zown[:, width:full] = total
        else:
            zsend[s - 1, :, zo_cols(s, 1)] = total.astype(bf16)
            zo_copy(s, 1).start()

    every = planes * group
    tiles = width // tile

    def weight_grads(t):
        cols = pl.ds(t * tile, tile)
        x_in = rows[:, :, :, :, cols].reshape(every, tile)
        after = pl.ds(width + t * tile, tile)
        g_in = rows[:, :, :, :, after].reshape(every, tile)
        both = contract(x_in, pre_all[...], 0, 0).astype(bf16)
        gg_ref[0, cols, :] = both[:, 0:half]
        ug_ref[0, cols, :] = both[:, half : 2 * half]
        dg_ref[0, :, cols] = contract(hidden_all[...], g_in, 0, 0).astype(bf16)

    def weights_ready():
        for load in loads[4:]:
            load.wait()

    relay(z, 0, lambda copy: copy.start())
    y_copy(0, 0).start()
    x_copy(0, 0).start()
    loads[2].wait()
    loads[3].wait()
    lane = lax.broadcasted_iota(jnp.int32, (tok_count, LANES), 1)
    ids, weights = ids_ref[...].T, rw_ref[...].T
    table = [jnp.zeros((tok_count, LANES), f32) for _ in range(3)]
    for k in range(ids.shape[1]):
        for part in range(3):
            hit = lane == ids[:, k : k + 1] + part * experts
            table[part] = jnp.where(hit, weights[:, k : k + 1], table[part])
    head = table[0].astype(bf16).astype(f32)
    mid = table[1] - table[1].astype(bf16).astype(f32)
    mid = mid.astype(bf16).astype(f32)
    rest = table[2] - table[2].astype(bf16).astype(f32)
    rest = rest - rest.astype(bf16).astype(f32)
    rows[z, c, 0, :, pl.ds(2 * width, LANES)] = (head + mid + rest).astype(bf16)
    loads[1].wait()
    relay(z, 1, lambda copy: copy.start())
    x_copy(0, 1).start()
    y_copy(0, 1).start()
    core_copy(0, 0, c).start()
    along(1, 0)
    pass_on(1, 0)
    across_y(0)
    across_x(0)
    along(1, 1)
    pass_on(1, 1)
    along(2, 0)
    to_core(0)
    pass_on(2, 0)
    gathered(0)
    along(2, 1)
    pass_on(2, 1)
    weights_ready()
    spread(0)
    across_y(1)
    across_x(1)
    forward(0)
    middle(0)
    spread(1)
    across_x(2)
    along(3, 0)
    pass_on(3, 0)
    across_y(2)
    to_core(2)
    to_core(1)
    gathered(1)
    along(3, 1)
    pass_on(3, 1)
    forward(1)
    middle(1)
    outward(1)
    gathered(2)
    across_x(3)
    inward(1, 0)
    inward(1, 1)
    across_y(3)
    reduce_left_half(1)
    forward(2)
    middle(2)
    outward(2)
    to_core(3)
    reduce_right_half(1)
    inward(2, 0)
    inward(2, 1)
    reduce_left_half(2)
    gathered(3)
    inward(0, 0)
    inward(0, 1)
    reduce_right_half(2)
    forward(3)
    middle(3)
    turn_right(1)
    inward(3, 0)
    inward(3, 1)
    turn_left(2)
    outward(3)
    turn_right(2)
    reduce_right_half(3)
    reduce_left_half(3)
    outward(0)
    collect_left(2)
    add_own()
    turn_right(3)
    collect_right(2)
    turn_left(1)
    turn_left(3)
    weight_grads(0)
    weight_grads(1)
    collect_right(1)
    reduce_own()
    collect_right(3)
    collect_left(1)
    collect_left(3)
    weight_grads(4)
    weight_grads(5)
    turn_right(0)
    turn_left(0)
    weight_grads(6)
    weight_grads(7)
    weight_grads(2)
    weight_grads(3)
    collect_left(0)
    collect_right(0)
    for s in range(planes):
        for k in range(2):
            x_copy(s, k).wait_send()
            y_copy(s, k).wait_send()
            swap_copy(s, k).wait_send()
            fa_copy(s, k).wait_send()
            fb_copy(s, k).wait_send()
            relay(plane(s), k, lambda copy: copy.wait_send())
            if s in WIDE_STEPS:
                wide_copy(s, k).wait_send()
        if s in EARLY_STEPS:
            early_copy(s).wait_send()
        xh_copy(s).wait_send()
        yh_copy(s).wait_send()
        for which in range(6):
            core_copy(s, which, c).wait_send()
        ta_copy(s).wait_send()
        tb_copy(s).wait_send()

    def total(k):
        out = zown[:, 0:width] if k == 0 else zown[:, width:full]
        ends = (width - thin[0], thin[1] - width)
        for s in range(1, planes):
            zo_copy(s, k).wait_recv()
            more = zrecv[s - 1, :, zo_cols(s, k)].astype(f32)
            if not whole(s):
                pad = jnp.zeros((tok_count, ends[k]), f32)
                more = jnp.concatenate([more, pad] if k == 0 else [pad, more], axis=1)
            out = out + more
        return out

    lo_ref[...] = total(0).astype(bf16)
    total_b = total(1)
    tg_ref[...] = total_b[:, 0:width].astype(bf16)
    marks = total_b[:, width:]
    routes = jnp.zeros((tok_count, LANES), f32)
    for k in range(ids.shape[1]):
        base = 2 * ids[:, k : k + 1]
        hit = (lane == base) | (lane == base + 1)
        hit = hit | (lane == base + LANES // 2) | (lane == base + LANES // 2 + 1)
        value = jnp.sum(jnp.where(hit, marks, 0.0), axis=1, keepdims=True)
        routes = jnp.where(lane == k, value, routes)
    rg_ref[...] = routes.T[0 : ids.shape[1], :]
    for s in range(1, planes):
        for k in range(2):
            zo_copy(s, k).wait_send()


def finish_kernel(
    lo_in, tg_in, rg_in, gg_in, ug_in, dg_in, lo_ref, tg_ref, rg_ref, gg_ref, ug_ref, dg_ref, out_sem, small_sem
):
    copies = []
    for i, (src, dst) in enumerate(((gg_in, gg_ref), (ug_in, ug_ref), (dg_in, dg_ref))):
        count = src.shape[1] // PARTS
        for j in range(PARTS):
            at = pl.ds(j * count, count)
            copies.append(pltpu.make_async_copy(src.at[0, at, :], dst.at[0, at, :], out_sem.at[i, j]))
    for i, (src, dst) in enumerate(((lo_in, lo_ref), (tg_in, tg_ref), (rg_in, rg_ref))):
        copies.append(pltpu.make_async_copy(src, dst, small_sem.at[i]))
    for copy in copies:
        copy.start()
    for copy in copies:
        copy.wait()


def kernel_body(tokens, expert_ids, route_weight, out_grad, gate_weight, up_weight, down_weight):
    dp_size, ex_size = lax.axis_size("dp"), lax.axis_size("expert")
    planes, experts = dp_size // 2, dp_size * ex_size // 2
    tok_count, width = tokens.shape
    half = gate_weight.shape[2]
    tile = TILE
    full = 2 * width + LANES
    wide = (width - WIDE[0], width + WIDE[1])
    thin = (width - THIN[0], width + THIN[1])
    bf16, f32 = jnp.bfloat16, jnp.float32
    every = planes * 8 * tok_count
    dma = pltpu.SemaphoreType.DMA
    vmem = pl.BlockSpec(memory_space=pltpu.VMEM)
    hbm = pl.BlockSpec(memory_space=pltpu.HBM)
    shape = jax.ShapeDtypeStruct
    several = lambda *counts: [dma(counts), dma(counts)]
    sems = [dma((7,)), dma((planes, 2, 2)), dma((planes, 2))]
    sems += several(planes, 2) * 2 + several(planes) * 2 + [dma((planes - 1, 2)), dma((planes, 2))]
    sems += several(planes, 6) + several(planes, 2) + several(planes) + several(planes, 2) * 2
    sems += several(planes) * 2 + several(planes - 1, 2)
    outs = pl.pallas_call(
        functools.partial(expert_kernel, planes, tok_count, width, half, experts, tile, wide, thin),
        out_shape=(
            pltpu.VMEM(tokens.shape, bf16),
            pltpu.VMEM(tokens.shape, bf16),
            pltpu.VMEM(route_weight.shape[::-1], f32),
            pltpu.VMEM(gate_weight.shape, bf16),
            pltpu.VMEM(up_weight.shape, bf16),
            pltpu.VMEM(down_weight.shape, bf16),
        ),
        in_specs=[hbm] * 7,
        out_specs=[vmem] * 6,
        scratch_shapes=[
            pltpu.VMEM(expert_ids.shape[::-1], jnp.int32),
            pltpu.VMEM(route_weight.shape[::-1], f32),
            pltpu.VMEM((planes, 2, 4, tok_count, full), bf16),
            pltpu.VMEM((planes, 2, 4, tok_count, full), bf16),
            pltpu.VMEM((planes, 4, tok_count, full), bf16),
            pltpu.VMEM((planes, 4, tok_count, full), bf16),
            pltpu.VMEM((planes, 4, tok_count, thin[1] - thin[0]), bf16),
            pltpu.VMEM((planes, 2, tok_count, width), bf16),
            pltpu.VMEM((planes, 2, tok_count, width + LANES), bf16),
            pltpu.VMEM((planes, tok_count, width), bf16),
            pltpu.VMEM((planes, tok_count, width + LANES), bf16),
            pltpu.VMEM((planes, tok_count, width), bf16),
            pltpu.VMEM((planes, tok_count, width + LANES), bf16),
            pltpu.VMEM((planes - 1, tok_count, full), bf16),
            pltpu.VMEM((planes - 1, tok_count, full), bf16),
            pltpu.VMEM((tok_count, full), f32),
            pltpu.VMEM((8 * tok_count, 2 * half), f32),
            pltpu.VMEM((every, half), bf16),
            pltpu.VMEM((every, 2 * half), bf16),
            pltpu.VMEM((width, 2 * half), bf16),
            pltpu.VMEM(down_weight.shape[1:], bf16),
        ] + sems,
        compiler_params=pltpu.CompilerParams(
            collective_id=0, has_side_effects=True, vmem_limit_bytes=60620 * 1024
        ),
    )(tokens, expert_ids.T, route_weight.T, out_grad, gate_weight, up_weight, down_weight)
    lo, tg, rg, gg, ug, dg = pl.pallas_call(
        finish_kernel,
        out_shape=tuple(shape(o.shape, o.dtype) for o in outs),
        in_specs=[vmem] * 6,
        out_specs=[hbm] * 6,
        scratch_shapes=[dma((3, PARTS)), dma((3,))],
        compiler_params=pltpu.CompilerParams(vmem_limit_bytes=4 * 1024 * 1024),
    )(*outs)
    return lo, tg, rg.T, gg, ug, dg


def solution(mesh):
    in_specs = (
        P(("dp", "expert"), None),
        P(("dp", "expert"), None),
        P(("dp", "expert"), None),
        P(("dp", "expert"), None),
        P(("dp", "expert"), None, None),
        P(("dp", "expert"), None, None),
        P(("dp", "expert"), None, None),
    )
    out_specs = (
        P(("dp", "expert"), None),
        P(("dp", "expert"), None),
        P(("dp", "expert"), None),
        P(("dp", "expert"), None, None),
        P(("dp", "expert"), None, None),
        P(("dp", "expert"), None, None),
    )
    dp_size, ex_size = mesh.shape["dp"], mesh.shape["expert"]
    pieces = dp_size * ex_size

    def step(tokens, expert_ids, *rest):
        capacity = 2 * (tokens.shape[0] * expert_ids.shape[1] // (pieces // 2))
        fits = ex_size == 4 and dp_size == 8 and 3 * pieces // 2 <= LANES
        fits = fits and pieces <= LANES // 2 and tokens.shape[1] % (2 * TILE) == 0
        fits = fits and tokens.shape[1] > max(WIDE + THIN)
        form = kernel_body if fits and capacity >= tokens.shape[0] else body
        return form(tokens, expert_ids, *rest)

    return jax.shard_map(step, mesh=mesh, in_specs=in_specs, out_specs=out_specs, check_vma=False)
```

```python
import functools

import jax
import jax.numpy as jnp
from jax import lax
from jax.experimental import pallas as pl
from jax.experimental.pallas import tpu as pltpu
from jax.sharding import PartitionSpec as P

LANES = 128
TILE = 256
PARTS = 1
WIDE = (256, 256)
WIDE_STEPS = (1, 2, 3)
THIN = (512, 512)
EARLY_STEPS = (1, 2)


def from_partner(shard, axis, apart):
    return lax.ppermute(shard, axis, [(i, i ^ 1 << apart) for i in range(lax.axis_size(axis))])


def contract(left_op, right_op, left_dim, right_dim):
    return lax.dot_general(
        left_op,
        right_op,
        (((left_dim,), (right_dim,)), ((), ())),
        preferred_element_type=jnp.float32,
    )


def deliver(buffer, dp_size, ex_size, experts, capacity, backward):
    feat_width = buffer.shape[1]
    doubled = jnp.broadcast_to(
        buffer.reshape(experts, 1, capacity, feat_width), (experts, 2, capacity, feat_width)
    )
    doubled = doubled.reshape(dp_size, ex_size, capacity, feat_width)
    if backward:
        arrived = lax.all_to_all(
            lax.all_to_all(doubled, "dp", split_axis=0, concat_axis=0, tiled=True),
            "expert",
            split_axis=1,
            concat_axis=1,
            tiled=True,
        )
    else:
        arrived = lax.all_to_all(
            lax.all_to_all(doubled, "dp", split_axis=0, concat_axis=0, tiled=True),
            "expert",
            split_axis=1,
            concat_axis=1,
            tiled=True,
        )
    return arrived.reshape(-1, feat_width)


def bring_back(partials_in, dp_size, ex_size, experts, capacity, half_index, backward):
    feat_width = partials_in.shape[1]
    if backward:
        partner = from_partner(partials_in, "expert", 0)
    else:
        partner = from_partner(partials_in, "expert", 0)
    summed = (partials_in.astype(jnp.float32) + partner.astype(jnp.float32)).astype(jnp.bfloat16)
    summed = summed.reshape(dp_size, ex_size, capacity, feat_width)
    own_half = lax.dynamic_slice_in_dim(summed, half_index * (capacity // 2), capacity // 2, 2)
    if backward:
        returned = lax.all_to_all(
            lax.all_to_all(own_half, "dp", split_axis=0, concat_axis=0, tiled=True),
            "expert",
            split_axis=1,
            concat_axis=1,
            tiled=True,
        )
    else:
        returned = lax.all_to_all(
            lax.all_to_all(own_half, "dp", split_axis=0, concat_axis=0, tiled=True),
            "expert",
            split_axis=1,
            concat_axis=1,
            tiled=True,
        )
    merged = returned.reshape(experts, capacity, feat_width)
    return merged.reshape(experts * capacity, feat_width)


def body(tokens, expert_ids, route_weight, out_grad, gate_weight, up_weight, down_weight):
    dp_size = lax.axis_size("dp")
    ex_size = lax.axis_size("expert")
    tok_count, feat_width = tokens.shape
    top_count = expert_ids.shape[1]
    experts = dp_size * ex_size // 2
    assigned = tok_count * top_count
    capacity = 2 * (assigned // experts)
    half_index = lax.axis_index("expert") % 2
    flat_ids = expert_ids.reshape(-1)
    order = jnp.arange(assigned, dtype=jnp.int32)
    earlier = (flat_ids[:, None] == flat_ids[None, :]) & (order[None, :] < order[:, None])
    slot_ids = jnp.sum(earlier.astype(jnp.int32), axis=1)
    place_row = flat_ids * capacity + slot_ids
    source = (
        jnp.full((experts * capacity,), -1, jnp.int32)
        .at[place_row]
        .set(jnp.arange(assigned, dtype=jnp.int32))
    )
    filled = source >= 0
    assign = jnp.maximum(source, 0)
    rows_tok = assign // top_count
    send_rows = jnp.where(filled[:, None], tokens[rows_tok], jnp.zeros((), jnp.bfloat16))
    in_rows = deliver(send_rows, dp_size, ex_size, experts, capacity, False)
    w_gate = gate_weight[0]
    w_up = up_weight[0]
    w_down = down_weight[0]
    gate_act = jnp.dot(in_rows, w_gate, preferred_element_type=jnp.float32)
    up_act = jnp.dot(in_rows, w_up, preferred_element_type=jnp.float32)
    sig_gate = jax.nn.sigmoid(gate_act)
    hidden = (gate_act * sig_gate * up_act).astype(jnp.bfloat16)
    partial_value = jnp.dot(hidden, w_down, preferred_element_type=jnp.float32).astype(jnp.bfloat16)
    expert_table = bring_back(partial_value, dp_size, ex_size, experts, capacity, half_index, False)
    expert_rows = expert_table[place_row].reshape(tok_count, top_count, feat_width)
    layer_out = jnp.sum(route_weight[:, :, None] * expert_rows.astype(jnp.float32), axis=1).astype(
        jnp.bfloat16
    )
    route_grad = jnp.einsum("tkd,td->tk", expert_rows, out_grad, preferred_element_type=jnp.float32)
    scaled = (route_weight[:, :, None] * out_grad[:, None, :].astype(jnp.float32)).astype(
        jnp.bfloat16
    )
    scaled = scaled.reshape(assigned, feat_width)
    send_grad = jnp.where(filled[:, None], scaled[assign], jnp.zeros((), jnp.bfloat16))
    grad_rows = deliver(send_grad, dp_size, ex_size, experts, capacity, True)
    hidden_grad = contract(grad_rows, w_down, 1, 1)
    gate_pre = (hidden_grad * up_act * sig_gate * (1.0 + gate_act * (1.0 - sig_gate))).astype(
        jnp.bfloat16
    )
    up_pre = (hidden_grad * gate_act * sig_gate).astype(jnp.bfloat16)
    partial_grad = (contract(gate_pre, w_gate, 1, 1) + contract(up_pre, w_up, 1, 1)).astype(
        jnp.bfloat16
    )
    gate_grad = contract(in_rows, gate_pre, 0, 0).astype(jnp.bfloat16)
    up_grad = contract(in_rows, up_pre, 0, 0).astype(jnp.bfloat16)
    down_grad = contract(hidden, grad_rows, 0, 0).astype(jnp.bfloat16)
    grad_table = bring_back(partial_grad, dp_size, ex_size, experts, capacity, half_index, True)
    expert_grad = grad_table[place_row].reshape(tok_count, top_count, feat_width)
    token_grad = jnp.sum(expert_grad.astype(jnp.float32), axis=1).astype(jnp.bfloat16)
    return (layer_out, token_grad, route_grad, gate_grad[None], up_grad[None], down_grad[None])


def expert_kernel(
    planes, tok_count, width, half, experts, tile, wide, thin,
    tok_hbm, ids_hbm, rw_hbm, og_hbm, wg_hbm, wu_hbm, wd_hbm,
    lo_ref, tg_ref, rg_ref, gg_ref, ug_ref, dg_ref,
    ids_ref, rw_ref, rows, parts, swapped, summed, early, first_a, first_b, turn_a, turn_b, second_a, second_b,
    zsend, zrecv, zown, act_ref, hidden_all, pre_all, wgu_ref, wd_ref,
    load_sem, z_ss, z_rs, x_ss, x_rs, y_ss, y_rs, xh_ss, xh_rs, yh_ss, yh_rs, wide_ss, wide_rs,
    core_ss, core_rs, swap_ss, swap_rs, early_ss, early_rs, fa_ss, fa_rs, fb_ss, fb_rs,
    ta_ss, ta_rs, tb_ss, tb_rs, zo_ss, zo_rs,
):
    f32, bf16 = jnp.float32, jnp.bfloat16
    dp, ex = lax.axis_index("dp"), lax.axis_index("expert")
    z, y, x, c = dp // 2, dp % 2, ex // 2, ex % 2
    piece = dp * lax.axis_size("expert") + ex
    mine = piece // 2
    full = 2 * width + LANES
    x_dev, y_dev, core_dev = (dp, (1 - x) * 2 + c), (z * 2 + 1 - y, ex), (dp, x * 2 + 1 - c)
    left, right = pl.ds(0, width), pl.ds(width, width + LANES)
    gather_mid = pl.ds(wide[0], wide[1] - wide[0])
    gather_left, gather_right = pl.ds(0, wide[0]), pl.ds(wide[1], full - wide[1])
    reduce_mid = pl.ds(thin[0], thin[1] - thin[0])
    reduce_left, reduce_right = pl.ds(0, thin[0]), pl.ds(thin[1], full - thin[1])
    packed_right = pl.ds(thin[0], full - thin[1])

    def remote(src, dst, send, recv, device):
        return pltpu.make_async_remote_copy(
            src_ref=src, dst_ref=dst, send_sem=send, recv_sem=recv,
            device_id=device, device_id_type=pl.DeviceIdType.MESH,
        )

    def plane(step):
        return z ^ step

    def z_peer(q):
        return (q * 2 + y, ex)

    own_left = rows.at[z, c, 0, :, left]
    own_right = rows.at[z, c, 0, :, pl.ds(width, width)]
    loads = [
        pltpu.make_async_copy(src, dst, load_sem.at[i])
        for i, (src, dst) in enumerate(
            (
                (tok_hbm, own_left), (og_hbm, own_right), (ids_hbm, ids_ref), (rw_hbm, rw_ref),
                (wg_hbm.at[0], wgu_ref.at[:, pl.ds(0, half)]), (wu_hbm.at[0], wgu_ref.at[:, pl.ds(half, half)]),
                (wd_hbm.at[0], wd_ref),
            )
        )
    ]
    for load in loads:
        load.start()

    barrier = pltpu.get_barrier_semaphore()
    peers = [x_dev, y_dev, core_dev]
    peers += [z_peer((z + d) % planes) for d in range(1, planes)]
    for peer in peers:
        pl.semaphore_signal(barrier, inc=1, device_id=peer, device_id_type=pl.DeviceIdType.MESH)

    loads[0].wait()
    pl.semaphore_wait(barrier, len(peers))

    def z_copy(q, way, k):
        part = rows.at[q, c, 0, :, (left, right)[k]]
        return remote(part, part, z_ss.at[q, way, k], z_rs.at[q, k], z_peer(z + 1 - 2 * way))

    def relay(q, k, run):
        @pl.when((q <= z) & (z < planes - 1))
        def _():
            run(z_copy(q, 0, k))

        @pl.when((q >= z) & (z > 0))
        def _():
            run(z_copy(q, 1, k))

    def z_landed(q, k):
        part = rows.at[q, c, 0, :, (left, right)[k]]
        remote(part, part, z_ss.at[q, 0, k], z_rs.at[q, k], core_dev).wait_recv()

    def along(away, k):
        @pl.when(z >= away)
        def _():
            z_landed(z - away, k)
            relay(z - away, k, lambda copy: copy.start())

        @pl.when(z < planes - away)
        def _():
            z_landed(z + away, k)
            relay(z + away, k, lambda copy: copy.start())

    def gather_cols(s, k):
        return ((gather_left, gather_right) if s in WIDE_STEPS else (left, right))[k]

    def x_copy(s, k):
        cols = gather_cols(s, k)
        src, dst = rows.at[plane(s), c, 0, :, cols], rows.at[plane(s), c, 1, :, cols]
        return remote(src, dst, x_ss.at[s, k], x_rs.at[s, k], x_dev)

    def y_copy(s, k):
        cols = gather_cols(s, k)
        src, dst = rows.at[plane(s), c, 0, :, cols], rows.at[plane(s), c, 2, :, cols]
        return remote(src, dst, y_ss.at[s, k], y_rs.at[s, k], y_dev)

    def xh_copy(s):
        cols = gather_cols(s, 0)
        src, dst = rows.at[plane(s), c, 2, :, cols], rows.at[plane(s), c, 3, :, cols]
        return remote(src, dst, xh_ss.at[s], xh_rs.at[s], x_dev)

    def yh_copy(s):
        cols = gather_cols(s, 1)
        src, dst = rows.at[plane(s), c, 1, :, cols], rows.at[plane(s), c, 3, :, cols]
        return remote(src, dst, yh_ss.at[s], yh_rs.at[s], y_dev)

    def wide_slots(q, k):
        return rows.at[q, c, (pl.ds(1, 2), pl.ds(3, 1))[k], :, gather_mid]

    def wide_copy(s, k):
        slots = wide_slots(z, k)
        return remote(slots, slots, wide_ss.at[s - 1, k], wide_rs.at[z, k], z_peer(plane(s)))

    def wide_landed(q, k):
        slots = wide_slots(q, k)
        remote(slots, slots, wide_ss.at[0, k], wide_rs.at[q, k], core_dev).wait_recv()

    def core_copy(s, which, core):
        slots, cols = (
            (pl.ds(0, 1), pl.ds(0, full)), (pl.ds(1, 2), gather_left), (pl.ds(1, 2), gather_right),
            (pl.ds(3, 1), gather_left), (pl.ds(3, 1), gather_right), (pl.ds(1, 3), gather_mid),
        )[which]
        ref = rows.at[plane(s), core, slots, :, cols]
        return remote(ref, ref, core_ss.at[s, which], core_rs.at[s, which], core_dev)

    def whole(s):
        return s not in EARLY_STEPS

    def swap_copy(s, k):
        cols = (left, right)[k]
        src, dst = parts.at[s, 1 - c, :, :, cols], swapped.at[s, :, :, cols]
        return remote(src, dst, swap_ss.at[s, k], swap_rs.at[s, k], core_dev)

    def early_copy(s):
        src = summed.at[s, :, :, reduce_mid]
        return remote(src, early.at[z], early_ss.at[s], early_rs.at[z], z_peer(plane(s)))

    def early_landed(q):
        remote(early.at[q], early.at[q], early_ss.at[0], early_rs.at[q], core_dev).wait_recv()

    def fa_copy(s, own):
        last = whole(s)
        cols = left if last else reduce_left
        src, dst = summed.at[s, 1 if own else 3, :, cols], first_a.at[s, own, :, cols]
        return remote(src, dst, fa_ss.at[s, own], fa_rs.at[s, own], x_dev)

    def fb_copy(s, own):
        last = whole(s)
        cols = right if last else reduce_right
        at = pl.ds(0, width + LANES) if last else pl.ds(thin[1] - width, full - thin[1])
        src, dst = summed.at[s, 2 if own else 3, :, cols], first_b.at[s, own, :, at]
        return remote(src, dst, fb_ss.at[s, own], fb_rs.at[s, own], y_dev)

    def ta_copy(s):
        last = whole(s)
        at = pl.ds(0, width if last else thin[0])
        src, dst = turn_a.at[s, :, at], second_a.at[s, :, at]
        return remote(src, dst, ta_ss.at[s], ta_rs.at[s], y_dev)

    def tb_copy(s):
        last = whole(s)
        at = pl.ds(0, width + LANES) if last else pl.ds(thin[1] - width, full - thin[1])
        src, dst = turn_b.at[s, :, at], second_b.at[s, :, at]
        return remote(src, dst, tb_ss.at[s], tb_rs.at[s], x_dev)

    def zo_cols(s, k):
        if whole(s):
            return (left, right)[k]
        return (pl.ds(0, thin[0]), packed_right)[k]

    def zo_copy(s, k):
        cols = zo_cols(s, k)
        src, dst = zsend.at[s - 1, :, cols], zrecv.at[s - 1, :, cols]
        return remote(src, dst, zo_ss.at[s - 1, k], zo_rs.at[s - 1, k], z_peer(plane(s)))

    def pass_on(s, k):
        x_copy(s, k).start()
        y_copy(s, k).start()
        if k == 1:
            core_copy(s, 0, c).start()

    def across_x(s):
        y_copy(s, 0).wait_recv()
        xh_copy(s).start()

    def across_y(s):
        x_copy(s, 1).wait_recv()
        yh_copy(s).start()

    def to_core(s):
        x_copy(s, 0).wait_recv()
        core_copy(s, 1, c).start()
        y_copy(s, 1).wait_recv()
        core_copy(s, 2, c).start()

    def gathered(s):
        xh_copy(s).wait_recv()
        core_copy(s, 3, c).start()
        yh_copy(s).wait_recv()
        core_copy(s, 4, c).start()
        if s in WIDE_STEPS:
            wide_landed(plane(s), 0)
            wide_landed(plane(s), 1)
        core_copy(s, 5, c).start()

    def spread(k):
        for s in WIDE_STEPS:
            wide_copy(s, k).start()

    group = 8 * tok_count
    glane = lax.broadcasted_iota(jnp.int32, (group, LANES), 1)

    def group_at(s):
        return pl.ds(pl.multiple_of(plane(s) * group, group), group)

    def forward(s):
        q = plane(s)
        for which in range(6):
            core_copy(s, which, 1 - c).wait_recv()
        x_in = rows[q, :, :, :, 0:width].reshape(group, width)
        act_ref[...] = contract(x_in, wgu_ref[...], 1, 0)

    def middle(s):
        q = plane(s)
        g_in = rows[q, :, :, :, width : 2 * width].reshape(group, width)
        back = contract(g_in, wd_ref[...], 1, 1)
        gate, up = act_ref[:, 0:half], act_ref[:, half : 2 * half]
        tab = rows[q, :, :, :, 2 * width : full].reshape(group, LANES).astype(f32)
        own = (glane == mine) | (glane == mine + experts) | (glane == mine + 2 * experts)
        weight = jnp.sum(jnp.where(own, tab, 0.0), axis=1, keepdims=True)
        sig = 1.0 / (1.0 + jnp.exp(-gate))
        act = gate * sig
        hidden = act * up
        route = jnp.sum(hidden * back, axis=1, keepdims=True)
        coarse = route.astype(bf16).astype(f32)
        fine = route - coarse
        marks = jnp.where(glane == piece, coarse, jnp.where(glane == piece + LANES // 2, fine, 0.0))
        parts[s, :, :, :, 2 * width : full] = marks.astype(bf16).reshape(2, 4, tok_count, LANES)
        back = weight * back
        hidden_all[group_at(s), :] = (weight * hidden).astype(bf16)
        pre_all[group_at(s), 0:half] = (back * up * sig * (1.0 + gate * (1.0 - sig))).astype(bf16)
        pre_all[group_at(s), half : 2 * half] = (back * act).astype(bf16)

    def outward(s):
        hid = hidden_all[group_at(s), :]
        for n in range(0, width, 2 * tile):
            cols = slice(n, n + 2 * tile)
            out = contract(hid, wd_ref[:, cols], 1, 0)
            parts[s, :, :, :, cols] = out.astype(bf16).reshape(2, 4, tok_count, 2 * tile)
        swap_copy(s, 0).start()

    def inward(s, part):
        pre = pre_all[group_at(s), :]
        for n in range(part * width // 2, (part + 1) * width // 2, 2 * tile):
            cols = slice(n, n + 2 * tile)
            grad = contract(pre, wgu_ref[cols, :], 1, 1)
            after = slice(width + n, width + n + 2 * tile)
            parts[s, :, :, :, after] = grad.astype(bf16).reshape(2, 4, tok_count, 2 * tile)
        if part == 1:
            swap_copy(s, 1).start()

    def add_slot(s, cols, t):
        total = parts[s, c, t, :, cols].astype(f32) + swapped[s, t, :, cols].astype(f32)
        summed[s, t, :, cols] = total.astype(bf16)

    def add_cores(s, cols):
        def add(t, carry):
            total = parts[s, c, t, :, cols].astype(f32) + swapped[s, t, :, cols].astype(f32)
            summed[s, t, :, cols] = total.astype(bf16)
            return carry

        lax.fori_loop(0, 4, add, 0)

    def reduce_left_half(s):
        swap_copy(s, 0).wait_recv()
        add_slot(s, left, 3)
        fa_copy(s, 0).start()
        add_slot(s, left, 1)
        fa_copy(s, 1).start()
        add_slot(s, left, 0)
        add_slot(s, left, 2)

    def reduce_right_half(s):
        swap_copy(s, 1).wait_recv()
        add_slot(s, right, 3)
        fb_copy(s, 0).start()
        add_slot(s, right, 2)
        fb_copy(s, 1).start()
        add_slot(s, right, 0)
        add_slot(s, right, 1)
        if s in EARLY_STEPS:
            early_copy(s).start()

    def add_own():
        swap_copy(0, 0).wait_recv()
        add_cores(0, reduce_left)
        swap_copy(0, 1).wait_recv()
        add_cores(0, reduce_right)

    def reduce_own():
        for s in EARLY_STEPS:
            early_landed(plane(s))

        def add(t, carry):
            total = parts[0, c, t, :, reduce_mid].astype(f32) + swapped[0, t, :, reduce_mid].astype(f32)
            for s in EARLY_STEPS:
                total = total + early[plane(s), t].astype(f32)
            summed[0, t, :, reduce_mid] = total.astype(bf16)
            return carry

        lax.fori_loop(0, 4, add, 0)
        for own in range(2):
            fa_copy(0, own).start()
            fb_copy(0, own).start()

    def turn_left(s):
        last = whole(s)
        fa_copy(s, 0).wait_recv()
        cols = slice(0, width if last else thin[0])
        total = summed[s, 2, :, cols].astype(f32) + first_a[s, 0, :, cols].astype(f32)
        turn_a[s, :, cols] = total.astype(bf16)
        ta_copy(s).start()

    def turn_right(s):
        last = whole(s)
        fb_copy(s, 0).wait_recv()
        begin = width if last else thin[1]
        at = slice(begin - width, full - width)
        total = summed[s, 1, :, begin:full].astype(f32) + first_b[s, 0, :, at].astype(f32)
        turn_b[s, :, at] = total.astype(bf16)
        tb_copy(s).start()

    def collect_left(s):
        fa_copy(s, 1).wait_recv()
        ta_copy(s).wait_recv()
        cols = slice(0, width if whole(s) else thin[0])
        total = summed[s, 0, :, cols].astype(f32) + first_a[s, 1, :, cols].astype(f32)
        total = total + second_a[s, :, cols].astype(f32)
        if s == 0:
            zown[:, cols] = total
        else:
            zsend[s - 1, :, cols] = total.astype(bf16)
            zo_copy(s, 0).start()

    def collect_right(s):
        fb_copy(s, 1).wait_recv()
        tb_copy(s).wait_recv()
        begin = width if whole(s) else thin[1]
        at = slice(begin - width, full - width)
        total = summed[s, 0, :, begin:full].astype(f32) + first_b[s, 1, :, at].astype(f32)
        total = total + second_b[s, :, at].astype(f32)
        if s == 0:
            zown[:, width:full] = total
        else:
            zsend[s - 1, :, zo_cols(s, 1)] = total.astype(bf16)
            zo_copy(s, 1).start()

    every = planes * group
    tiles = width // tile

    def weight_grads(t):
        cols = pl.ds(t * tile, tile)
        x_in = rows[:, :, :, :, cols].reshape(every, tile)
        after = pl.ds(width + t * tile, tile)
        g_in = rows[:, :, :, :, after].reshape(every, tile)
        both = contract(x_in, pre_all[...], 0, 0).astype(bf16)
        gg_ref[0, cols, :] = both[:, 0:half]
        ug_ref[0, cols, :] = both[:, half : 2 * half]
        dg_ref[0, :, cols] = contract(hidden_all[...], g_in, 0, 0).astype(bf16)

    def weights_ready():
        for load in loads[4:]:
            load.wait()

    relay(z, 0, lambda copy: copy.start())
    y_copy(0, 0).start()
    x_copy(0, 0).start()
    loads[2].wait()
    loads[3].wait()
    lane = lax.broadcasted_iota(jnp.int32, (tok_count, LANES), 1)
    ids, weights = ids_ref[...].T, rw_ref[...].T
    table = [jnp.zeros((tok_count, LANES), f32) for _ in range(3)]
    for k in range(ids.shape[1]):
        for part in range(3):
            hit = lane == ids[:, k : k + 1] + part * experts
            table[part] = jnp.where(hit, weights[:, k : k + 1], table[part])
    head = table[0].astype(bf16).astype(f32)
    mid = table[1] - table[1].astype(bf16).astype(f32)
    mid = mid.astype(bf16).astype(f32)
    rest = table[2] - table[2].astype(bf16).astype(f32)
    rest = rest - rest.astype(bf16).astype(f32)
    rows[z, c, 0, :, pl.ds(2 * width, LANES)] = (head + mid + rest).astype(bf16)
    loads[1].wait()
    relay(z, 1, lambda copy: copy.start())
    x_copy(0, 1).start()
    y_copy(0, 1).start()
    core_copy(0, 0, c).start()
    along(1, 0)
    pass_on(1, 0)
    across_y(0)
    across_x(0)
    along(1, 1)
    pass_on(1, 1)
    along(2, 0)
    to_core(0)
    pass_on(2, 0)
    gathered(0)
    along(2, 1)
    pass_on(2, 1)
    weights_ready()
    spread(0)
    across_y(1)
    across_x(1)
    forward(0)
    middle(0)
    spread(1)
    across_x(2)
    along(3, 0)
    pass_on(3, 0)
    across_y(2)
    to_core(2)
    to_core(1)
    gathered(1)
    along(3, 1)
    pass_on(3, 1)
    forward(1)
    middle(1)
    outward(1)
    gathered(2)
    across_x(3)
    inward(1, 0)
    inward(1, 1)
    across_y(3)
    reduce_left_half(1)
    forward(2)
    middle(2)
    outward(2)
    to_core(3)
    reduce_right_half(1)
    inward(2, 0)
    inward(2, 1)
    reduce_left_half(2)
    gathered(3)
    inward(0, 0)
    inward(0, 1)
    reduce_right_half(2)
    forward(3)
    middle(3)
    turn_right(1)
    inward(3, 0)
    inward(3, 1)
    turn_left(2)
    outward(3)
    turn_right(2)
    reduce_right_half(3)
    reduce_left_half(3)
    outward(0)
    collect_left(2)
    add_own()
    turn_right(3)
    collect_right(2)
    turn_left(1)
    turn_left(3)
    weight_grads(0)
    weight_grads(1)
    collect_right(1)
    reduce_own()
    collect_right(3)
    collect_left(1)
    collect_left(3)
    weight_grads(4)
    weight_grads(5)
    turn_right(0)
    turn_left(0)
    weight_grads(6)
    weight_grads(7)
    weight_grads(2)
    weight_grads(3)
    collect_left(0)
    collect_right(0)
    for s in range(planes):
        for k in range(2):
            x_copy(s, k).wait_send()
            y_copy(s, k).wait_send()
            swap_copy(s, k).wait_send()
            fa_copy(s, k).wait_send()
            fb_copy(s, k).wait_send()
            relay(plane(s), k, lambda copy: copy.wait_send())
            if s in WIDE_STEPS:
                wide_copy(s, k).wait_send()
        if s in EARLY_STEPS:
            early_copy(s).wait_send()
        xh_copy(s).wait_send()
        yh_copy(s).wait_send()
        for which in range(6):
            core_copy(s, which, c).wait_send()
        ta_copy(s).wait_send()
        tb_copy(s).wait_send()

    def total(k):
        out = zown[:, 0:width] if k == 0 else zown[:, width:full]
        ends = (width - thin[0], thin[1] - width)
        for s in range(1, planes):
            zo_copy(s, k).wait_recv()
            more = zrecv[s - 1, :, zo_cols(s, k)].astype(f32)
            if not whole(s):
                pad = jnp.zeros((tok_count, ends[k]), f32)
                more = jnp.concatenate([more, pad] if k == 0 else [pad, more], axis=1)
            out = out + more
        return out

    lo_ref[...] = total(0).astype(bf16)
    total_b = total(1)
    tg_ref[...] = total_b[:, 0:width].astype(bf16)
    marks = total_b[:, width:]
    routes = jnp.zeros((tok_count, LANES), f32)
    for k in range(ids.shape[1]):
        base = 2 * ids[:, k : k + 1]
        hit = (lane == base) | (lane == base + 1)
        hit = hit | (lane == base + LANES // 2) | (lane == base + LANES // 2 + 1)
        value = jnp.sum(jnp.where(hit, marks, 0.0), axis=1, keepdims=True)
        routes = jnp.where(lane == k, value, routes)
    rg_ref[...] = routes.T[0 : ids.shape[1], :]
    for s in range(1, planes):
        for k in range(2):
            zo_copy(s, k).wait_send()


def finish_kernel(
    lo_in, tg_in, rg_in, gg_in, ug_in, dg_in, lo_ref, tg_ref, rg_ref, gg_ref, ug_ref, dg_ref, out_sem, small_sem
):
    copies = []
    for i, (src, dst) in enumerate(((gg_in, gg_ref), (ug_in, ug_ref), (dg_in, dg_ref))):
        count = src.shape[1] // PARTS
        for j in range(PARTS):
            at = pl.ds(j * count, count)
            copies.append(pltpu.make_async_copy(src.at[0, at, :], dst.at[0, at, :], out_sem.at[i, j]))
    for i, (src, dst) in enumerate(((lo_in, lo_ref), (tg_in, tg_ref), (rg_in, rg_ref))):
        copies.append(pltpu.make_async_copy(src, dst, small_sem.at[i]))
    for copy in copies:
        copy.start()
    for copy in copies:
        copy.wait()


def kernel_body(tokens, expert_ids, route_weight, out_grad, gate_weight, up_weight, down_weight):
    dp_size, ex_size = lax.axis_size("dp"), lax.axis_size("expert")
    planes, experts = dp_size // 2, dp_size * ex_size // 2
    tok_count, width = tokens.shape
    half = gate_weight.shape[2]
    tile = TILE
    full = 2 * width + LANES
    wide = (width - WIDE[0], width + WIDE[1])
    thin = (width - THIN[0], width + THIN[1])
    bf16, f32 = jnp.bfloat16, jnp.float32
    every = planes * 8 * tok_count
    dma = pltpu.SemaphoreType.DMA
    vmem = pl.BlockSpec(memory_space=pltpu.VMEM)
    hbm = pl.BlockSpec(memory_space=pltpu.HBM)
    shape = jax.ShapeDtypeStruct
    several = lambda *counts: [dma(counts), dma(counts)]
    sems = [dma((7,)), dma((planes, 2, 2)), dma((planes, 2))]
    sems += several(planes, 2) * 2 + several(planes) * 2 + [dma((planes - 1, 2)), dma((planes, 2))]
    sems += several(planes, 6) + several(planes, 2) + several(planes) + several(planes, 2) * 2
    sems += several(planes) * 2 + several(planes - 1, 2)
    outs = pl.pallas_call(
        functools.partial(expert_kernel, planes, tok_count, width, half, experts, tile, wide, thin),
        out_shape=(
            pltpu.VMEM(tokens.shape, bf16),
            pltpu.VMEM(tokens.shape, bf16),
            pltpu.VMEM(route_weight.shape[::-1], f32),
            pltpu.VMEM(gate_weight.shape, bf16),
            pltpu.VMEM(up_weight.shape, bf16),
            pltpu.VMEM(down_weight.shape, bf16),
        ),
        in_specs=[hbm] * 7,
        out_specs=[vmem] * 6,
        scratch_shapes=[
            pltpu.VMEM(expert_ids.shape[::-1], jnp.int32),
            pltpu.VMEM(route_weight.shape[::-1], f32),
            pltpu.VMEM((planes, 2, 4, tok_count, full), bf16),
            pltpu.VMEM((planes, 2, 4, tok_count, full), bf16),
            pltpu.VMEM((planes, 4, tok_count, full), bf16),
            pltpu.VMEM((planes, 4, tok_count, full), bf16),
            pltpu.VMEM((planes, 4, tok_count, thin[1] - thin[0]), bf16),
            pltpu.VMEM((planes, 2, tok_count, width), bf16),
            pltpu.VMEM((planes, 2, tok_count, width + LANES), bf16),
            pltpu.VMEM((planes, tok_count, width), bf16),
            pltpu.VMEM((planes, tok_count, width + LANES), bf16),
            pltpu.VMEM((planes, tok_count, width), bf16),
            pltpu.VMEM((planes, tok_count, width + LANES), bf16),
            pltpu.VMEM((planes - 1, tok_count, full), bf16),
            pltpu.VMEM((planes - 1, tok_count, full), bf16),
            pltpu.VMEM((tok_count, full), f32),
            pltpu.VMEM((8 * tok_count, 2 * half), f32),
            pltpu.VMEM((every, half), bf16),
            pltpu.VMEM((every, 2 * half), bf16),
            pltpu.VMEM((width, 2 * half), bf16),
            pltpu.VMEM(down_weight.shape[1:], bf16),
        ] + sems,
        compiler_params=pltpu.CompilerParams(
            collective_id=0, has_side_effects=True, vmem_limit_bytes=60620 * 1024
        ),
    )(tokens, expert_ids.T, route_weight.T, out_grad, gate_weight, up_weight, down_weight)
    lo, tg, rg, gg, ug, dg = pl.pallas_call(
        finish_kernel,
        out_shape=tuple(shape(o.shape, o.dtype) for o in outs),
        in_specs=[vmem] * 6,
        out_specs=[hbm] * 6,
        scratch_shapes=[dma((3, PARTS)), dma((3,))],
        compiler_params=pltpu.CompilerParams(vmem_limit_bytes=4 * 1024 * 1024),
    )(*outs)
    return lo, tg, rg.T, gg, ug, dg


def solution(mesh):
    in_specs = (
        P(("dp", "expert"), None),
        P(("dp", "expert"), None),
        P(("dp", "expert"), None),
        P(("dp", "expert"), None),
        P(("dp", "expert"), None, None),
        P(("dp", "expert"), None, None),
        P(("dp", "expert"), None, None),
    )
    out_specs = (
        P(("dp", "expert"), None),
        P(("dp", "expert"), None),
        P(("dp", "expert"), None),
        P(("dp", "expert"), None, None),
        P(("dp", "expert"), None, None),
        P(("dp", "expert"), None, None),
    )
    dp_size, ex_size = mesh.shape["dp"], mesh.shape["expert"]
    pieces = dp_size * ex_size

    def step(tokens, expert_ids, *rest):
        capacity = 2 * (tokens.shape[0] * expert_ids.shape[1] // (pieces // 2))
        fits = ex_size == 4 and dp_size == 8 and 3 * pieces // 2 <= LANES
        fits = fits and pieces <= LANES // 2 and tokens.shape[1] % (2 * TILE) == 0
        fits = fits and tokens.shape[1] > max(WIDE + THIN)
        form = kernel_body if fits and capacity >= tokens.shape[0] else body
        return form(tokens, expert_ids, *rest)

    return jax.shard_map(step, mesh=mesh, in_specs=in_specs, out_specs=out_specs, check_vma=False)
```
